32 devices in a mesh: rep: 2 (over x), atom: 16 (over z, y, core).
Axes of the slice: x: 2, y: 2, z: 4, core: 2. Of those that a mesh axis runs over, the one named last changes fastest.
Arguments:
- features: bfloat16 [4096, 256], P(('rep', 'atom')), parts along dimension 0, may hold values from -6 to 6
- fractional: float32 [3, 4096], P(None, ('rep', 'atom')), parts along dimension 1, may hold values from 0 to 1, as said below
- distances: float32 [64, 4096], P(None, ('rep', 'atom')), parts along dimension 1, may hold values from 0.8 to 4.8
- neighbours: int32 [64, 4096], P(None, ('rep', 'atom')), parts along dimension 1, may hold values from 0 to 383
- edge_mask: int32 [64, 4096], P(None, ('rep', 'atom')), parts along dimension 1, may hold values 0 or 1
- wave_index: int32 [3, 2048], replicated, may hold values from -6 to 6
- w_rbf: bfloat16 [2, 64, 512], replicated, may hold values from -1.5 to 1.5
- w_filter: bfloat16 [2, 512, 256], replicated, may hold values from -0.25 to 0.25
- w_mixing: bfloat16 [2, 256, 256], replicated, may hold values from -0.375 to 0.375
- w_short: bfloat16 [2, 256, 256], replicated, may hold values from -0.375 to 0.375
- w_long: bfloat16 [2, 256, 256], replicated, may hold values from -0.375 to 0.375
Outputs:
- features_out: bfloat16 [4096, 256], P(('rep', 'atom')), parts along dimension 0
The draws below stay inside these ranges and needn't reach their ends.
There are 2 independent parts, one for each index of `rep`. The reference program is written for one: setup_inputs(seed, part) draws one part's arguments, and reference() takes and returns one part's arrays. A program takes and returns all parts, laid end to end along the dimension named above; an argument that names none is the same for every part. Nothing has to cross between parts.
Inputs may be any that keep to these rules, and one draw needn't show every extreme that they name: neighbours[n, i] indexes the concatenation of the previous brick, atom i's own brick and the next brick, cyclic over the 16 bricks. `fractional`: atom i has its z coordinate within brick i // 128, that is between (i // 128) * 128 / 2048 and one brick further.
All inputs are finite; a program needn't handle non-finite values. No bound on the sum of `edge_mask` on one device may be relied on, other than what follows from the above.
Results may differ from the reference program's by a relative error of at most 0.01.
Values may be sent and summed in bfloat16 or wider, within the bound.
A program may use at most 64 MiB of HBM per device.

```python
import math
import jax
import jax.numpy as jnp
from jax import lax

F = 256
H = 512
R = 64
K = 2048
NB = 64
LAYERS = 2
ATOM_DEV = 128
ATOMS = 2048


def draw_fractional(key, part):
    base = jax.random.fold_in(key, 7)
    first, second = jax.random.split(base)
    plane = jax.random.uniform(first, (2, ATOMS), jnp.float32)
    offset = jax.random.uniform(second, (ATOMS,), jnp.float32)
    brick = (jnp.arange(ATOMS) // ATOM_DEV).astype(jnp.float32)
    height = (brick + offset) * (ATOM_DEV / ATOMS)
    return jnp.concatenate([plane, height[None, :]], axis=0)


def with_ends(result, stream_key, least, high):
    dims = result.shape
    spot = [jax.random.randint(jax.random.fold_in(stream_key, axis), (), 0, dims[axis]) for axis in range(len(dims))]
    result = result.at[tuple(spot)].set(least)
    longest = dims.index(max(dims))
    spot[longest] = (spot[longest] + 1) % dims[longest]
    return result.at[tuple(spot)].set(high)


def block_scale(key, extent, cuts, low, largest):
    gain = 1.0
    for axis_at, parts in cuts:
        heights = jax.random.uniform(jax.random.fold_in(jax.random.fold_in(key, 6), axis_at), (parts,), jnp.float32, low / len(cuts), largest / len(cuts))
        gain = gain * jnp.repeat(jnp.exp(heights), extent[axis_at] // parts).reshape((-1,) + (1,) * (len(extent) - 1 - axis_at))
    return gain


def scatter_about(key, extent, scale, limit, cuts=(), held_as=jnp.bfloat16):
    drawn = jax.random.normal(key, extent, jnp.float32) * scale
    if len(cuts) > 0:
        drawn = block_scale(key, extent, cuts, -0.22, 0.18) * drawn
    return jnp.clip(drawn, min=-limit, max=limit).astype(held_as)


def setup_inputs(seed: int = 0, part: int = 0) -> dict:
    seeds = jax.random.split(jax.random.key(seed), 12)
    own_keys = jax.random.split(jax.random.fold_in(seeds[11], part), 12)
    return {
        "features": scatter_about(own_keys[0], (ATOMS, F), 1.0, 6.0, ((0, 16),)),
        "fractional": draw_fractional(jax.random.fold_in(jax.random.fold_in(seeds[11], part), 71), part),
        "distances": jnp.clip(0.8 + 4 * jax.random.uniform(own_keys[2], (NB, ATOMS), jnp.float32) ** block_scale(own_keys[2], (NB, ATOMS), ((1, 16),), -0.2, 0.2), 0.8, 4.8),
        "neighbours": with_ends(jax.random.randint(own_keys[3], (NB, ATOMS), 0, 3 * ATOM_DEV), jax.random.fold_in(own_keys[3], 1), 0, (3 * ATOM_DEV) - 1).astype(jnp.int32),
        "edge_mask": with_ends((jax.random.randint(own_keys[4], (NB, ATOMS), 0, 4) < 3).astype(jnp.int32), jax.random.fold_in(own_keys[4], 1), 0, 1),
        "wave_index": with_ends(jax.random.randint(seeds[5], (3, K), -6, 7), jax.random.fold_in(seeds[5], 1), -6, 6).astype(jnp.int32),
        "w_rbf": scatter_about(seeds[6], (LAYERS, R, H), (R // 4) ** -0.5, 1.5),
        "w_filter": scatter_about(seeds[7], (LAYERS, H, F), H ** -0.5, 0.25),
        "w_mixing": scatter_about(seeds[8], (LAYERS, F, F), F ** -0.5, 0.375),
        "w_short": scatter_about(seeds[9], (LAYERS, F, F), F ** -0.5, 0.375),
        "w_long": scatter_about(seeds[10], (LAYERS, F, F), F ** -0.5, 0.375),
    }


slot_group = 8
tau_value = 2.0 * math.pi

def edge_basis(distance, count):
    centers = 0.5 + 4.5 * jnp.arange(count, dtype=jnp.float32) / (count - 1)
    offset = distance[..., None] - centers
    return jnp.exp(-4.0 * offset * offset).astype(jnp.bfloat16)

def envelope(distance):
    return 0.5 * (jnp.cos(math.pi * distance / 5.0) + 1.0)

def messages(table, index, distance, edge_weight, rbf_weight, filter_weight):
    groups = index.shape[0] // slot_group
    rows = index.shape[1]
    count = rbf_weight.shape[0]

    def advance(total, pieces):
        index_part, distance_part, weight_part = pieces
        basis = edge_basis(distance_part, count).reshape(slot_group * rows, count)
        inner = jax.nn.silu(jnp.dot(basis, rbf_weight, preferred_element_type=jnp.float32)).astype(jnp.bfloat16)
        filters = jnp.dot(inner, filter_weight, preferred_element_type=jnp.float32).reshape(slot_group, rows, -1)
        filters = filters * weight_part[:, :, None]
        gathered = jnp.take(table, index_part, axis=0).astype(jnp.float32)
        return (total + lax.optimization_barrier(jnp.sum(filters * gathered, axis=0)), None)
    start = jnp.zeros((rows, filter_weight.shape[1]), jnp.float32)
    total, _ = lax.scan(advance, start, (index.reshape(groups, slot_group, rows), distance.reshape(groups, slot_group, rows), edge_weight.reshape(groups, slot_group, rows)))
    return total

def transposed(left, right):
    return lax.dot_general(left, right, (((0,), (0,)), ((), ())), preferred_element_type=jnp.float32)

def reference(features, fractional, distances, neighbours, edge_mask, wave_index, w_rbf, w_filter, w_mixing, w_short, w_long):
    atoms_all = features.shape[0]
    width = features.shape[1]
    brick_start = (jnp.arange(atoms_all, dtype=jnp.int32) // ATOM_DEV * ATOM_DEV).astype(jnp.int32)
    partner = ((brick_start[None, :] - ATOM_DEV + neighbours) % atoms_all).astype(jnp.int32)
    edge_weight = envelope(distances) * edge_mask.astype(jnp.float32)
    wave_float = wave_index.astype(jnp.float32)
    angle = tau_value * (fractional[0][:, None] * wave_float[0][None, :] + fractional[1][:, None] * wave_float[1][None, :] + fractional[2][:, None] * wave_float[2][None, :])
    cosine = jnp.cos(angle).astype(jnp.bfloat16)
    sine = jnp.sin(angle).astype(jnp.bfloat16)
    gains = 1.0 / (1.0 + (wave_float[0] * wave_float[0] + wave_float[1] * wave_float[1] + wave_float[2] * wave_float[2]) / 16.0)
    state = features
    for layer_index in range(LAYERS):
        message = messages(state, partner, distances, edge_weight, w_rbf[layer_index], w_filter[layer_index]).astype(jnp.bfloat16)
        structure = jnp.concatenate([transposed(cosine, state), transposed(sine, state)], axis=1)
        scaled = (structure * gains[:, None] / jnp.sqrt(jnp.float32(atoms_all))).astype(jnp.bfloat16)
        waves = scaled.shape[0]
        potential = jnp.dot(scaled.reshape(2 * waves, width), w_mixing[layer_index], preferred_element_type=jnp.float32)
        potential = potential.reshape(waves, 2 * width).astype(jnp.bfloat16)
        field = jnp.dot(cosine, potential[:, :width], preferred_element_type=jnp.float32)
        field = field + jnp.dot(sine, potential[:, width:], preferred_element_type=jnp.float32)
        field = (field * (4.0 / math.sqrt(K))).astype(jnp.bfloat16)
        update = jnp.dot(message, w_short[layer_index], preferred_element_type=jnp.float32)
        update = update + jnp.dot(field, w_long[layer_index], preferred_element_type=jnp.float32)
        state = (state.astype(jnp.float32) + jax.nn.silu(update)).astype(jnp.bfloat16)
    return state
```

```python
import functools
import math

import jax
import jax.numpy as jnp
import numpy as np
from jax import lax
from jax.experimental import pallas as pl
from jax.experimental.pallas import tpu as pltpu
from jax.sharding import PartitionSpec as P

MOST = 6
PAIRS = 88
SIDE = 2 * MOST + 1
GROUP = 8
MESH = pl.DeviceIdType.MESH


def fitted(function, terms):
    at = np.cos(np.pi * (np.arange(400) + 0.5) / 400) * 0.125 + 0.125
    values = function(np.sqrt(at))
    series = np.polynomial.chebyshev.Chebyshev.fit(at, values, terms - 1, domain=[0.0, 0.25])
    return [float(c) for c in series.convert(kind=np.polynomial.Polynomial).coef]


COS = fitted(lambda r: np.cos(2 * np.pi * r), 9)
SIN = fitted(lambda r: np.sin(2 * np.pi * r) / r, 8)


def horner(coefficients, x):
    total = jnp.full_like(x, coefficients[-1])
    for c in coefficients[-2::-1]:
        total = total * x + c
    return total


def cos_sin(turn):
    r = turn - jnp.floor(turn + 0.5)
    square = r * r
    return horner(COS, square), horner(SIN, square) * r


def pair_orders(shape):
    p = lax.broadcasted_iota(jnp.int32, shape, 0).astype(jnp.float32)
    row = jnp.floor((p - (MOST + 0.5)) * (1.0 / SIDE))
    m0 = row + 1.0
    m1 = jnp.where(m0 > 0.5, p - (MOST + 1) - row * SIDE - MOST, p)
    return m0, m1


def wave_weights(wave, scale):
    m0, m1, m2 = wave[0:1, :], wave[1:2, :], wave[2:3, :]
    flip = (m0 < 0) | ((m0 == 0) & (m1 < 0))
    m0, m1, m2 = (jnp.where(flip, -m, m) for m in (m0, m1, m2))
    pair = jnp.where(m0 == 0, m1, (MOST + 1) + (m0 - 1) * SIDE + m1 + MOST)
    many = wave.shape[1]
    one_pair = pair == lax.broadcasted_iota(jnp.int32, (PAIRS, many), 0)
    one_z = (m2 + 8) == lax.broadcasted_iota(jnp.int32, (16, many), 0)
    count = lax.dot_general(
        jnp.where(one_pair, 1.0, 0.0).astype(jnp.bfloat16),
        jnp.where(one_z, 1.0, 0.0).astype(jnp.bfloat16),
        (((1,), (1,)), ((), ())),
        preferred_element_type=jnp.float32,
    )
    n0, n1 = pair_orders((PAIRS, 16))
    n2 = lax.broadcasted_iota(jnp.int32, (PAIRS, 16), 1).astype(jnp.float32) - 8.0
    return count * scale / (1.0 + (n0 * n0 + n1 * n1 + n2 * n2) / 16.0)


def wave_rows(fraction, weight):
    width = fraction.shape[1]
    m0, m1 = pair_orders((PAIRS, width))
    cp, sp = cos_sin(m0 * fraction[0:1, :] + m1 * fraction[1:2, :])
    m2 = lax.broadcasted_iota(jnp.int32, (8, width), 0).astype(jnp.float32)
    cz, sz = cos_sin(m2 * fraction[2:3, :])

    def block(m, rows):
        if weight is not None:
            rows = [w * r for w, r in zip(m, rows)]
        return jnp.concatenate(rows, axis=0).astype(jnp.bfloat16)

    def factor(m):
        return None if weight is None else weight[:, 8 + m : 9 + m]

    yield 0, block((factor(0),) * 2, [cp, sp])
    for m in range(1, MOST + 1):
        c, s = cz[m : m + 1, :], sz[m : m + 1, :]
        a, b, g, h = cp * c, sp * s, sp * c, cp * s
        up, down = factor(m), factor(-m)
        yield 2 * PAIRS * (2 * m - 1), block((up, up, down, down), [a - b, g + h, a + b, g - h])


def step_kernel(
    grid, scale,
    features, fractional, distances, neighbours, edge_mask, wave_index,
    w_rbf, w_filter, w_mixing, w_short, w_long,
    out_ref,
    dist_v, neigh_v, mask_v, wave_v, rbf_v, filter_v, mixing_v, short_v, long_v,
    rbf_t, filter_t, both, weight_v, near16, edge_v,
    source_x, target_x, source_rows, target_rows, matrix,
    states, beside, table, filters, partial, own_part, arrived, message,
    in_sem, near_send, near_recv, col_send, col_recv, row_send, row_recv,
    place_send, place_recv,
):
    across, along = grid
    bricks = across * along
    layers = w_rbf.shape[0]
    slots, rows = distances.shape
    count, hidden = w_rbf.shape[1:]
    width = w_filter.shape[2]
    me = lax.axis_index("atom")
    a, b = me // along, lax.rem(me, along)
    after = lax.rem(me + 1, bricks)
    before = lax.rem(me + bricks - 1, bricks)

    def column(k):
        return lax.rem(a + k, across) * along + b

    def line(k):
        return a * along + lax.rem(b + k, along)

    def to(index):
        return {"atom": index}

    peers = [column(k) for k in range(1, across)] + [line(k) for k in range(1, along)]
    peers += [before, after]
    barrier = pltpu.get_barrier_semaphore()
    for peer in peers:
        pl.semaphore_signal(barrier, inc=1, device_id=to(peer), device_id_type=MESH)

    loads = [
        (distances, dist_v), (w_rbf, rbf_v), (w_filter, filter_v), (wave_index, wave_v),
        (features, states.at[0, 0]), (fractional, source_x.at[0]), (fractional, target_x.at[0]),
        (neighbours, neigh_v), (edge_mask, mask_v), (w_mixing, mixing_v), (w_long, long_v),
        (w_short, short_v),
    ]
    loads = [pltpu.make_async_copy(x, y, in_sem.at[i]) for i, (x, y) in enumerate(loads)]
    for load in loads:
        load.start()
    pl.semaphore_wait(barrier, len(peers))

    def remote(source, target, send, recv, index):
        return pltpu.make_async_remote_copy(
            src_ref=source, dst_ref=target, send_sem=send, recv_sem=recv,
            device_id=to(index), device_id_type=MESH,
        )

    def send_states(layer, source):
        near = [
            remote(source, beside.at[layer, 0], near_send.at[layer, 0], near_recv.at[layer, 0], after),
            remote(source, beside.at[layer, 1], near_send.at[layer, 1], near_recv.at[layer, 1], before),
        ]
        far = [
            remote(
                source, states.at[layer, k], col_send.at[layer, k], col_recv.at[layer, k], column(k)
            )
            for k in range(1, across)
        ]
        for copy in near + far:
            copy.start()
        return near, far

    placed = [
        remote(fractional, source_x.at[k], place_send.at[0, k], place_recv.at[0, k], column(k))
        for k in range(1, across)
    ] + [
        remote(fractional, target_x.at[k], place_send.at[1, k], place_recv.at[1, k], line(k))
        for k in range(1, along)
    ]
    for copy in placed:
        copy.start()
    near, far = send_states(0, features)

    def transposed(x):
        return x.astype(jnp.float32).T.astype(jnp.bfloat16)

    center = 0.5 + 4.5 * lax.broadcasted_iota(jnp.int32, (count, rows), 0).astype(jnp.float32) / (
        count - 1
    )

    def edge_filters(layer):
        rbf_t[...] = transposed(rbf_v[layer].astype(jnp.float32) * 0.5)
        filter_t[...] = transposed(filter_v[layer])
        for first in range(0, slots, GROUP):
            parts = []
            for slot in range(first, first + GROUP):
                offset = dist_v[slot : slot + 1, :] - center
                parts.append(jnp.exp(-4.0 * offset * offset).astype(jnp.bfloat16))
            half = jnp.dot(
                rbf_t[...], jnp.concatenate(parts, axis=1), preferred_element_type=jnp.float32
            )
            inner = (half + half * jnp.tanh(half)).astype(jnp.bfloat16)
            filters[:, first * rows : (first + GROUP) * rows] = jnp.dot(
                filter_t[...], inner, preferred_element_type=jnp.float32
            ).astype(jnp.bfloat16)

    place = lax.broadcasted_iota(jnp.int32, (3 * rows, rows), 0).astype(jnp.int16)

    def gather(first, last):
        total = message[...]
        for begin in range(first, last, GROUP):
            picks = []
            for slot in range(begin, begin + GROUP):
                hit = place == near16[slot : slot + 1, :]
                picks.append(jnp.where(hit, jnp.bfloat16(1), jnp.bfloat16(0)))
            gathered = jnp.dot(
                table[...], jnp.concatenate(picks, axis=1), preferred_element_type=jnp.float32
            )
            for at in range(GROUP):
                slot = begin + at
                factor = filters[:, slot * rows : (slot + 1) * rows].astype(jnp.float32)
                factor = factor * edge_v[slot : slot + 1, :]
                total = total + gathered[:, at * rows : (at + 1) * rows] * factor
        message[...] = total

    def send_partial(layer):
        held = [states[layer, k] for k in range(across)]
        product = jnp.dot(
            matrix[...], jnp.concatenate(held, axis=0), preferred_element_type=jnp.float32
        )
        copies = []
        for k in range(1, along):
            partial[layer, k] = product[k * rows : (k + 1) * rows, :].astype(jnp.bfloat16)
            copies.append(
                remote(
                    partial.at[layer, k], arrived.at[layer, k], row_send.at[layer, k],
                    row_recv.at[layer, k], line(k),
                )
            )
            copies[-1].start()
        own_part[...] = product[0:rows, :]
        return copies

    def update(layer):
        field = own_part[...]
        for k in range(1, along):
            field = field + arrived[layer, k].astype(jnp.float32)
        short = jnp.dot(
            message[...].T.astype(jnp.bfloat16), short_v[layer], preferred_element_type=jnp.float32
        )
        step = short + jnp.dot(
            field.astype(jnp.bfloat16), both[layer], preferred_element_type=jnp.float32
        )
        state = states[layer, 0].astype(jnp.float32) + step * jax.nn.sigmoid(step)
        return state.astype(jnp.bfloat16)

    for load in loads[:4]:
        load.wait()
    edge_filters(0)

    for load in loads[4:]:
        load.wait()
    for copy in placed:
        copy.wait_recv()
    weight_v[...] = wave_weights(wave_v[...], scale)
    weight = weight_v[...]

    def sources(k, carry):
        for row, block in wave_rows(source_x[k], None):
            source_rows[row : row + block.shape[0], pl.ds(pl.multiple_of(k * rows, rows), rows)] = block
        return carry

    def targets(k, carry):
        at = lax.rem(along - k, along)
        for row, block in wave_rows(target_x[at], weight):
            target_rows[row : row + block.shape[0], pl.ds(pl.multiple_of(k * rows, rows), rows)] = block
        return carry

    lax.fori_loop(0, across, sources, 0)
    lax.fori_loop(0, along, targets, 0)
    matrix[...] = lax.dot_general(
        target_rows[...], source_rows[...], (((0,), (0,)), ((), ())),
        preferred_element_type=jnp.float32,
    ).astype(jnp.bfloat16)
    for layer in range(layers):
        both[layer] = jnp.dot(
            mixing_v[layer], long_v[layer], preferred_element_type=jnp.float32
        ).astype(jnp.bfloat16)
    near16[...] = neigh_v[...].astype(jnp.int16)
    envelope = 0.5 * (cos_sin(dist_v[...] * 0.1)[0] + 1.0)
    edge_v[...] = envelope * mask_v[...].astype(jnp.float32)

    sent = list(placed)
    for layer in range(layers):
        if layer > 0:
            edge_filters(layer)
        message[...] = jnp.zeros_like(message)
        for copy in near:
            copy.wait_recv()
        table[:, 0:rows] = transposed(beside[layer, 0])
        table[:, rows : 2 * rows] = transposed(states[layer, 0])
        table[:, 2 * rows : 3 * rows] = transposed(beside[layer, 1])
        if layer > 0:
            gather(0, slots // 2)
        for copy in far:
            copy.wait_recv()
        copies = send_partial(layer)
        gather(slots // 2 if layer > 0 else 0, slots)
        for copy in copies:
            copy.wait_recv()
        sent += near + far + copies
        state = update(layer)
        if layer + 1 < layers:
            states[layer + 1, 0] = state
            near, far = send_states(layer + 1, states.at[layer + 1, 0])
        else:
            out_ref[...] = state
    for copy in sent:
        copy.wait_send()


def per_device(
    features, fractional, distances, neighbours, edge_mask, wave_index,
    w_rbf, w_filter, w_mixing, w_short, w_long,
):
    bricks = lax.axis_size("atom")
    along = max(n for n in range(1, bricks + 1) if bricks % n == 0 and n * n <= bricks)
    across = bricks // along
    rows, width = features.shape
    slots = distances.shape[0]
    layers, count, hidden = w_rbf.shape
    scale = 4.0 / math.sqrt(wave_index.shape[1]) / math.sqrt(rows * bricks)
    waves = 2 * PAIRS * SIDE
    half, full = jnp.bfloat16, jnp.float32
    dma = pltpu.SemaphoreType.DMA
    V = pltpu.VMEM
    scratch = [
        V(distances.shape, full), V(neighbours.shape, jnp.int32), V(edge_mask.shape, jnp.int32),
        V(wave_index.shape, jnp.int32), V(w_rbf.shape, half), V(w_filter.shape, half),
        V(w_mixing.shape, half), V(w_short.shape, half), V(w_long.shape, half),
        V((hidden, count), half), V((width, hidden), half), V((layers, width, width), half),
        V((PAIRS, 16), full), V((slots, rows), jnp.int16), V((slots, rows), full),
        V((across,) + fractional.shape, full), V((along,) + fractional.shape, full),
        V((waves, across * rows), half), V((waves, along * rows), half),
        V((along * rows, across * rows), half),
        V((layers, across, rows, width), half), V((layers, 2, rows, width), half),
        V((width, 3 * rows), half), V((width, slots * rows), half),
        V((layers, along, rows, width), half), V((rows, width), full),
        V((layers, along, rows, width), half), V((width, rows), full),
        dma((12,)), dma((layers, 2)), dma((layers, 2)),
        dma((layers, across)), dma((layers, across)), dma((layers, along)), dma((layers, along)),
        dma((2, max(across, along))), dma((2, max(across, along))),
    ]
    return pl.pallas_call(
        functools.partial(step_kernel, (across, along), scale),
        out_shape=jax.ShapeDtypeStruct(features.shape, features.dtype),
        in_specs=[pl.BlockSpec(memory_space=pl.ANY)] * 11,
        out_specs=pl.BlockSpec(memory_space=pltpu.VMEM),
        scratch_shapes=scratch,
        compiler_params=pltpu.CompilerParams(
            collective_id=0, has_side_effects=True, vmem_limit_bytes=60 << 20
        ),
        name="step",
    )(
        features, fractional, distances, neighbours, edge_mask, wave_index,
        w_rbf, w_filter, w_mixing, w_short, w_long,
    )


def solution(mesh):
    split_rows = P(("rep", "atom"), None)
    split_columns = P(None, ("rep", "atom"))
    in_specs = (split_rows,) + (split_columns,) * 4 + (P(),) * 6
    return jax.shard_map(
        per_device, mesh=mesh, in_specs=in_specs, out_specs=split_rows, check_vma=False
    )
```

```python
import functools
import math

import jax
import jax.numpy as jnp
import numpy as np
from jax import lax
from jax.experimental import pallas as pl
from jax.experimental.pallas import tpu as pltpu
from jax.sharding import PartitionSpec as P

MOST = 6
PAIRS = 88
SIDE = 2 * MOST + 1
GROUP = 8
EARLY, MIDDLE, PRE, SECOND, LATER = 1, 3, 7, 2, 0
MESH = pl.DeviceIdType.MESH


def fitted(function, terms):
    at = np.cos(np.pi * (np.arange(400) + 0.5) / 400) * 0.125 + 0.125
    values = function(np.sqrt(at))
    series = np.polynomial.chebyshev.Chebyshev.fit(at, values, terms - 1, domain=[0.0, 0.25])
    return [float(c) for c in series.convert(kind=np.polynomial.Polynomial).coef]


COS = fitted(lambda r: np.cos(2 * np.pi * r), 9)
SIN = fitted(lambda r: np.sin(2 * np.pi * r) / r, 8)


def horner(coefficients, x):
    total = jnp.full_like(x, coefficients[-1])
    for c in coefficients[-2::-1]:
        total = total * x + c
    return total


def cos_sin(turn):
    r = turn - jnp.floor(turn + 0.5)
    square = r * r
    return horner(COS, square), horner(SIN, square) * r


def pair_orders(shape):
    p = lax.broadcasted_iota(jnp.int32, shape, 0).astype(jnp.float32)
    row = jnp.floor((p - (MOST + 0.5)) * (1.0 / SIDE))
    m0 = row + 1.0
    m1 = jnp.where(m0 > 0.5, p - (MOST + 1) - row * SIDE - MOST, p)
    return m0, m1


def wave_weights(wave, scale):
    m0, m1, m2 = wave[0:1, :], wave[1:2, :], wave[2:3, :]
    flip = (m0 < 0) | ((m0 == 0) & (m1 < 0))
    m0, m1, m2 = (jnp.where(flip, -m, m) for m in (m0, m1, m2))
    pair = jnp.where(m0 == 0, m1, (MOST + 1) + (m0 - 1) * SIDE + m1 + MOST)
    many = wave.shape[1]
    one_pair = pair == lax.broadcasted_iota(jnp.int32, (PAIRS, many), 0)
    one_z = (m2 + 8) == lax.broadcasted_iota(jnp.int32, (16, many), 0)
    count = lax.dot_general(
        jnp.where(one_pair, 1.0, 0.0).astype(jnp.bfloat16),
        jnp.where(one_z, 1.0, 0.0).astype(jnp.bfloat16),
        (((1,), (1,)), ((), ())),
        preferred_element_type=jnp.float32,
    )
    n0, n1 = pair_orders((PAIRS, 16))
    n2 = lax.broadcasted_iota(jnp.int32, (PAIRS, 16), 1).astype(jnp.float32) - 8.0
    return count * scale / (1.0 + (n0 * n0 + n1 * n1 + n2 * n2) / 16.0)


def wave_rows(fraction, orders, weights):
    width = fraction.shape[1]
    cp, sp = cos_sin(orders[0] * fraction[0:1, :] + orders[1] * fraction[1:2, :])
    m2 = lax.broadcasted_iota(jnp.int32, (8, width), 0).astype(jnp.float32)
    cz, sz = cos_sin(m2 * fraction[2:3, :])
    for m in range(MOST + 1):
        if m == 0:
            signs, terms = (0, 0), (cp, sp)
        else:
            c, s = cz[m : m + 1, :], sz[m : m + 1, :]
            x, y, u, v = cp * c, sp * s, sp * c, cp * s
            signs, terms = (m, m, -m, -m), (x - y, u + v, x + y, u - v)
        row = 2 * PAIRS * max(2 * m - 1, 0)
        forms = [terms]
        if weights is not None:
            forms.append([weights[MOST + at] * term for at, term in zip(signs, terms)])
        yield row, [jnp.concatenate(form, axis=0).astype(jnp.bfloat16) for form in forms]


def step_kernel(
    grid, scale,
    features, fractional, distances, neighbours, edge_mask, wave_index,
    w_rbf, w_filter, w_mixing, w_short, w_long,
    out_ref,
    dist_v, neigh_v, mask_v, wave_v, rbf_v, filter_v, mixing_v, short_v, long_v,
    rbf_t, filter_t, both, orders, weights, near16, edge_v,
    source_x, target_x, source_rows, target_rows, target_t, matrix, flipped,
    own, beside, line_held, plane_held, table, filters,
    plane_part, line_part, plane_got, line_got, own_field, message,
    in_sem, near_send, near_recv, line_send, line_recv, plane_send, plane_recv,
    place_send, place_recv,
):
    across, along = grid
    bricks = across * along
    layers = w_rbf.shape[0]
    slots, rows = distances.shape
    count, hidden = w_rbf.shape[1:]
    width = w_filter.shape[2]
    half = width // 2
    me = lax.axis_index("atom")
    a, b = me // along, lax.rem(me, along)
    after = lax.rem(me + 1, bricks)
    before = lax.rem(me + bricks - 1, bricks)

    def line(k):
        return lax.rem(a + k, across) * along + b

    def plane(k):
        return a * along + lax.rem(b + k, along)

    def to(index):
        return {"atom": index}

    peers = [line(k) for k in range(1, across)] + [plane(k) for k in range(1, along)]
    peers += [before, after]
    barrier = pltpu.get_barrier_semaphore()
    for peer in peers:
        pl.semaphore_signal(barrier, inc=1, device_id=to(peer), device_id_type=MESH)

    loads = [
        (distances, dist_v), (w_rbf, rbf_v), (w_filter, filter_v),
        (features.at[:, 0:half], own.at[0, 0]), (features.at[:, half:width], own.at[0, 1]),
        (fractional, source_x.at[0]), (fractional, target_x.at[0]), (wave_index, wave_v),
        (neighbours, neigh_v), (edge_mask, mask_v), (w_mixing, mixing_v), (w_long, long_v),
        (w_short, short_v),
    ]
    loads = [pltpu.make_async_copy(x, y, in_sem.at[i]) for i, (x, y) in enumerate(loads)]
    for load in loads:
        load.start()

    def remote(source, target, send, recv, index):
        return pltpu.make_async_remote_copy(
            src_ref=source, dst_ref=target, send_sem=send, recv_sem=recv,
            device_id=to(index), device_id_type=MESH,
        )

    def send_states(layer):
        far = [
            remote(
                own.at[layer, 0], line_held.at[layer, k], line_send.at[layer, 0, k],
                line_recv.at[layer, 0, k], line(k),
            )
            for k in range(1, across)
        ] + [
            remote(
                own.at[layer, 1], plane_held.at[layer, k], plane_send.at[layer, 0, k],
                plane_recv.at[layer, 0, k], plane(k),
            )
            for k in range(1, along)
        ]
        near, cross = [], []
        for at, index in enumerate((after, before)):
            for part in range(2):
                copy = remote(
                    own.at[layer, part], beside.at[layer, at, part], near_send.at[layer, at, part],
                    near_recv.at[layer, at, part], index,
                )
                (cross if part else near).append(copy)
        for copy in far:
            copy.start()
        return near, cross, far

    first, last = b == 0, b == along - 1
    sends, takes = (last, first), (first, last)

    def start_near(near, cross):
        for at in range(2):
            near[at].start()
            pl.when(sends[at])(cross[at].start)

    def wait_near(near, cross):
        for at in range(2):
            near[at].wait_recv()
            pl.when(takes[at])(cross[at].wait_recv)

    def end_near(near, cross):
        for at in range(2):
            near[at].wait_send()
            pl.when(sends[at])(cross[at].wait_send)

    def transposed(x):
        return x.astype(jnp.float32).T.astype(jnp.bfloat16)

    center = 0.5 + 4.5 * lax.broadcasted_iota(jnp.int32, (count, rows), 0).astype(jnp.float32) / (
        count - 1
    )
    blocks = slots // GROUP

    def edge_weights(layer):
        rbf_t[layer] = transposed(rbf_v[layer].astype(jnp.float32) * 0.5)
        filter_t[layer] = transposed(filter_v[layer])

    def edge_filters(layer, begin, end):
        for first in range(begin * GROUP, end * GROUP, GROUP):
            parts = []
            for slot in range(first, first + GROUP):
                offset = dist_v[slot : slot + 1, :] - center
                parts.append(jnp.exp(-4.0 * offset * offset).astype(jnp.bfloat16))
            hidden_half = jnp.dot(
                rbf_t[layer], jnp.concatenate(parts, axis=1), preferred_element_type=jnp.float32
            )
            inner = (hidden_half + hidden_half * jnp.tanh(hidden_half)).astype(jnp.bfloat16)
            filters[layer, :, first * rows : (first + GROUP) * rows] = jnp.dot(
                filter_t[layer], inner, preferred_element_type=jnp.float32
            ).astype(jnp.bfloat16)

    place = lax.broadcasted_iota(jnp.int32, (3 * rows, rows), 0).astype(jnp.int16)

    def gather(layer, begin, end):
        total = message[...]
        for first in range(begin * GROUP, end * GROUP, GROUP):
            picks = []
            for slot in range(first, first + GROUP):
                hit = place == near16[slot : slot + 1, :]
                picks.append(jnp.where(hit, jnp.bfloat16(1), jnp.bfloat16(0)))
            gathered = jnp.dot(
                table[...], jnp.concatenate(picks, axis=1), preferred_element_type=jnp.float32
            )
            for at in range(GROUP):
                slot = first + at
                factor = filters[layer, :, slot * rows : (slot + 1) * rows].astype(jnp.float32)
                factor = factor * edge_v[slot : slot + 1, :]
                total = total + gathered[:, at * rows : (at + 1) * rows] * factor
        message[...] = total

    def send_partial(layer):
        held = [own[layer, 0]] + [line_held[layer, k] for k in range(1, across)]
        down = jnp.dot(
            matrix[...], jnp.concatenate(held, axis=0), preferred_element_type=jnp.float32
        )
        held = [own[layer, 1]] + [plane_held[layer, along - k] for k in range(1, along)]
        up = jnp.dot(
            flipped[...], jnp.concatenate(held, axis=0), preferred_element_type=jnp.float32
        )
        copies = []
        for k in range(1, across):
            line_part[layer, k] = up[k * rows : (k + 1) * rows, :].astype(jnp.bfloat16)
            copies.append(
                remote(
                    line_part.at[layer, k], line_got.at[layer, k], line_send.at[layer, 1, k],
                    line_recv.at[layer, 1, k], line(across - k),
                )
            )
        for k in range(1, along):
            plane_part[layer, k] = down[k * rows : (k + 1) * rows, :].astype(jnp.bfloat16)
            copies.append(
                remote(
                    plane_part.at[layer, k], plane_got.at[layer, k], plane_send.at[layer, 1, k],
                    plane_recv.at[layer, 1, k], plane(k),
                )
            )
        for copy in copies:
            copy.start()
        own_field[0] = down[0:rows, :]
        own_field[1] = up[0:rows, :]
        return copies

    def update(layer):
        short = jnp.dot(
            message[...].T.astype(jnp.bfloat16), short_v[layer], preferred_element_type=jnp.float32
        )
        left, right = own_field[0], own_field[1]
        for k in range(1, along):
            left = left + plane_got[layer, k].astype(jnp.float32)
        for k in range(1, across):
            right = right + line_got[layer, k].astype(jnp.float32)
        field = jnp.concatenate([left, right], axis=1).astype(jnp.bfloat16)
        step = short + jnp.dot(field, both[layer], preferred_element_type=jnp.float32)
        state = jnp.concatenate([own[layer, 0], own[layer, 1]], axis=1).astype(jnp.float32)
        return (state + step * jax.nn.sigmoid(step)).astype(jnp.bfloat16)

    def fill_table(layer):
        def put(at, part, ref):
            table[part * half : (part + 1) * half, at * rows : (at + 1) * rows] = transposed(ref[...])

        put(0, 0, beside.at[layer, 0, 0])
        put(1, 0, own.at[layer, 0])
        put(1, 1, own.at[layer, 1])
        put(2, 0, beside.at[layer, 1, 0])
        for at, slot in ((0, 1 % along), (1, along - 1)):
            pl.when(takes[at])(functools.partial(put, 2 * at, 1, beside.at[layer, at, 1]))
            pl.when(jnp.logical_not(takes[at]))(
                functools.partial(put, 2 * at, 1, plane_held.at[layer, slot])
            )

    done = [0] * (layers + 1)

    def fill(layer, end):
        if layer < layers and done[layer] < end:
            if done[layer] == 0:
                edge_weights(layer)
            edge_filters(layer, done[layer], end)
            done[layer] = end

    for load in loads[:3]:
        load.wait()
    fill(0, EARLY)
    for load in loads[3:7]:
        load.wait()
    pl.semaphore_wait(barrier, len(peers))
    placed_plane = [
        remote(fractional, target_x.at[k], place_send.at[1, k], place_recv.at[1, k], plane(k))
        for k in range(1, along)
    ]
    placed_line = [
        remote(fractional, source_x.at[k], place_send.at[0, k], place_recv.at[0, k], line(k))
        for k in range(1, across)
    ]
    for copy in placed_line + placed_plane:
        copy.start()
    near, cross, far = send_states(0)
    for load in loads[7:]:
        load.wait()
    weight = wave_weights(wave_v[...], scale)
    for m in range(-MOST, MOST + 1):
        weights[MOST + m] = jnp.broadcast_to(weight[:, 8 + m : 9 + m], (PAIRS, rows))
    for at, order in enumerate(pair_orders((PAIRS, rows))):
        orders[at] = order
    for row, (plain, weighted) in wave_rows(source_x[0], orders, weights):
        source_rows[row : row + plain.shape[0], 0:rows] = plain
        target_rows[row : row + plain.shape[0], 0:rows] = weighted
    fill(0, MIDDLE)
    start_near(near, cross)
    for layer in range(layers):
        both[layer] = jnp.dot(
            mixing_v[layer], long_v[layer], preferred_element_type=jnp.float32
        ).astype(jnp.bfloat16)
    near16[...] = neigh_v[...].astype(jnp.int16)
    envelope = 0.5 * (cos_sin(dist_v[...] * 0.1)[0] + 1.0)
    edge_v[...] = envelope * mask_v[...].astype(jnp.float32)
    fill(0, PRE)

    def lanes(k):
        return pl.ds(pl.multiple_of(k * rows, rows), rows)

    def sources(k, carry):
        for row, (plain,) in wave_rows(source_x[k], orders, None):
            source_rows[row : row + plain.shape[0], lanes(k)] = plain
        return carry

    def targets(k, carry):
        for row, (_, weighted) in wave_rows(target_x[along - k], orders, weights):
            target_rows[row : row + weighted.shape[0], lanes(k)] = weighted
        return carry

    for copy in placed_plane:
        copy.wait_recv()
    lax.fori_loop(1, along, targets, 0)
    target_t[...] = target_rows[...].T
    for copy in placed_line:
        copy.wait_recv()
    lax.fori_loop(1, across, sources, 0)
    product = jnp.dot(target_t[...], source_rows[...], preferred_element_type=jnp.float32)
    matrix[...] = product.astype(jnp.bfloat16)
    flipped[...] = product.T.astype(jnp.bfloat16)

    sent = placed_line + placed_plane
    for layer in range(layers):
        message[...] = jnp.zeros_like(message)
        if layer > 0:
            fill(layer, min(done[layer] + LATER, blocks))
            start_near(near, cross)
            fill(layer, blocks)
        for copy in far:
            copy.wait_recv()
        copies = send_partial(layer)
        fill(layer, blocks)
        wait_near(near, cross)
        fill_table(layer)
        gather(layer, 0, blocks)
        fill(layer + 1, SECOND)
        for copy in copies:
            copy.wait_recv()
        sent += far + copies
        state = update(layer)
        end_near(near, cross)
        if layer + 1 < layers:
            own[layer + 1, 0] = state[:, 0:half]
            own[layer + 1, 1] = state[:, half:width]
            near, cross, far = send_states(layer + 1)
        else:
            out_ref[...] = state
    for copy in sent:
        copy.wait_send()


def per_device(
    features, fractional, distances, neighbours, edge_mask, wave_index,
    w_rbf, w_filter, w_mixing, w_short, w_long,
):
    bricks = lax.axis_size("atom")
    along = max(n for n in range(1, bricks + 1) if bricks % n == 0 and n * n <= bricks)
    across = bricks // along
    rows, width = features.shape
    slots = distances.shape[0]
    layers, count, hidden = w_rbf.shape
    scale = 4.0 / math.sqrt(wave_index.shape[1]) / math.sqrt(rows * bricks)
    waves = 2 * PAIRS * SIDE
    half, full = jnp.bfloat16, jnp.float32
    dma = pltpu.SemaphoreType.DMA
    V = pltpu.VMEM
    part = (rows, width // 2)
    scratch = [
        V(distances.shape, full), V(neighbours.shape, jnp.int32), V(edge_mask.shape, jnp.int32),
        V(wave_index.shape, jnp.int32), V(w_rbf.shape, half), V(w_filter.shape, half),
        V(w_mixing.shape, half), V(w_short.shape, half), V(w_long.shape, half),
        V((layers, hidden, count), half), V((layers, width, hidden), half),
        V((layers, width, width), half),
        V((2, PAIRS, rows), full), V((SIDE, PAIRS, rows), full), V((slots, rows), jnp.int16), V((slots, rows), full),
        V((across,) + fractional.shape, full), V((along,) + fractional.shape, full),
        V((waves, across * rows), half), V((waves, along * rows), half),
        V((along * rows, waves), half),
        V((along * rows, across * rows), half), V((across * rows, along * rows), half),
        V((layers, 2) + part, half), V((layers, 2, 2) + part, half),
        V((layers, across) + part, half), V((layers, along) + part, half),
        V((width, 3 * rows), half), V((layers, width, slots * rows), half),
        V((layers, along) + part, half), V((layers, across) + part, half),
        V((layers, along) + part, half), V((layers, across) + part, half),
        V((2,) + part, full), V((width, rows), full),
        dma((13,)), dma((layers, 2, 2)), dma((layers, 2, 2)),
        dma((layers, 2, across)), dma((layers, 2, across)),
        dma((layers, 2, along)), dma((layers, 2, along)),
        dma((2, max(across, along))), dma((2, max(across, along))),
    ]
    return pl.pallas_call(
        functools.partial(step_kernel, (across, along), scale),
        out_shape=jax.ShapeDtypeStruct(features.shape, features.dtype),
        in_specs=[pl.BlockSpec(memory_space=pl.ANY)] * 11,
        out_specs=pl.BlockSpec(memory_space=pltpu.VMEM),
        scratch_shapes=scratch,
        compiler_params=pltpu.CompilerParams(
            collective_id=0, has_side_effects=True, vmem_limit_bytes=60 << 20
        ),
        name="step",
    )(
        features, fractional, distances, neighbours, edge_mask, wave_index,
        w_rbf, w_filter, w_mixing, w_short, w_long,
    )


def solution(mesh):
    split_rows = P(("rep", "atom"), None)
    split_columns = P(None, ("rep", "atom"))
    in_specs = (split_rows,) + (split_columns,) * 4 + (P(),) * 6
    return jax.shard_map(
        per_device, mesh=mesh, in_specs=in_specs, out_specs=split_rows, check_vma=False
    )
```

```python
import functools
import math

import jax
import jax.numpy as jnp
import numpy as np
from jax import lax
from jax.experimental import pallas as pl
from jax.experimental.pallas import tpu as pltpu
from jax.sharding import PartitionSpec as P

MOST = 6
PAIRS = 88
SIDE = 2 * MOST + 1
GROUP = 8
EARLY, MIDDLE, PRE, SECOND, LATER = 1, 2, 5, 1, 0
MESH = pl.DeviceIdType.MESH


def fitted(function, terms):
    at = np.cos(np.pi * (np.arange(400) + 0.5) / 400) * 0.125 + 0.125
    values = function(np.sqrt(at))
    series = np.polynomial.chebyshev.Chebyshev.fit(at, values, terms - 1, domain=[0.0, 0.25])
    return [float(c) for c in series.convert(kind=np.polynomial.Polynomial).coef]


COS = fitted(lambda r: np.cos(2 * np.pi * r), 9)
SIN = fitted(lambda r: np.sin(2 * np.pi * r) / r, 8)


def horner(coefficients, x):
    total = jnp.full_like(x, coefficients[-1])
    for c in coefficients[-2::-1]:
        total = total * x + c
    return total


def cos_sin(turn):
    r = turn - jnp.floor(turn + 0.5)
    square = r * r
    return horner(COS, square), horner(SIN, square) * r


def pair_orders(shape):
    p = lax.broadcasted_iota(jnp.int32, shape, 0).astype(jnp.float32)
    row = jnp.floor((p - (MOST + 0.5)) * (1.0 / SIDE))
    m0 = row + 1.0
    m1 = jnp.where(m0 > 0.5, p - (MOST + 1) - row * SIDE - MOST, p)
    return m0, m1


def wave_weights(wave, scale):
    m0, m1, m2 = wave[0:1, :], wave[1:2, :], wave[2:3, :]
    flip = (m0 < 0) | ((m0 == 0) & (m1 < 0))
    m0, m1, m2 = (jnp.where(flip, -m, m) for m in (m0, m1, m2))
    pair = jnp.where(m0 == 0, m1, (MOST + 1) + (m0 - 1) * SIDE + m1 + MOST)
    many = wave.shape[1]
    one_pair = pair == lax.broadcasted_iota(jnp.int32, (PAIRS, many), 0)
    one_z = (m2 + 8) == lax.broadcasted_iota(jnp.int32, (16, many), 0)
    count = lax.dot_general(
        jnp.where(one_pair, 1.0, 0.0).astype(jnp.bfloat16),
        jnp.where(one_z, 1.0, 0.0).astype(jnp.bfloat16),
        (((1,), (1,)), ((), ())),
        preferred_element_type=jnp.float32,
    )
    n0, n1 = pair_orders((PAIRS, 16))
    n2 = lax.broadcasted_iota(jnp.int32, (PAIRS, 16), 1).astype(jnp.float32) - 8.0
    return count * scale / (1.0 + (n0 * n0 + n1 * n1 + n2 * n2) / 16.0)


def wave_rows(fraction, orders, weights):
    width = fraction.shape[1]
    cp, sp = cos_sin(orders[0] * fraction[0:1, :] + orders[1] * fraction[1:2, :])
    m2 = lax.broadcasted_iota(jnp.int32, (8, width), 0).astype(jnp.float32)
    cz, sz = cos_sin(m2 * fraction[2:3, :])
    for m in range(MOST + 1):
        if m == 0:
            signs, terms = (0, 0), (cp, sp)
        else:
            c, s = cz[m : m + 1, :], sz[m : m + 1, :]
            x, y, u, v = cp * c, sp * s, sp * c, cp * s
            signs, terms = (m, m, -m, -m), (x - y, u + v, x + y, u - v)
        row = 2 * PAIRS * max(2 * m - 1, 0)
        forms = [terms]
        if weights is not None:
            forms.append([weights[MOST + at] * term for at, term in zip(signs, terms)])
        yield row, [jnp.concatenate(form, axis=0).astype(jnp.bfloat16) for form in forms]


def step_kernel(
    grid, scale,
    features, fractional, distances, neighbours, edge_mask, wave_index,
    w_rbf, w_filter, w_mixing, w_short, w_long,
    out_ref,
    dist_v, neigh_v, mask_v, wave_v, rbf_v, filter_v, mixing_v, short_v, long_v,
    rbf_t, filter_t, both, orders, weights, near16, edge_v,
    source_x, target_x, source_rows, target_rows, target_t, matrix, flipped,
    own, beside, line_held, plane_held, table, filters,
    plane_part, line_part, plane_got, line_got, own_field, message,
    in_sem, near_send, near_recv, line_send, line_recv, plane_send, plane_recv,
    place_send, place_recv,
):
    across, along = grid
    bricks = across * along
    layers = w_rbf.shape[0]
    slots, rows = distances.shape
    count, hidden = w_rbf.shape[1:]
    width = w_filter.shape[2]
    half = width // 2
    me = lax.axis_index("atom")
    a, b = me // along, lax.rem(me, along)
    after = lax.rem(me + 1, bricks)
    before = lax.rem(me + bricks - 1, bricks)

    def line(k):
        return lax.rem(a + k, across) * along + b

    def plane(k):
        return a * along + lax.rem(b + k, along)

    def to(index):
        return {"atom": index}

    peers = [line(k) for k in range(1, across)] + [plane(k) for k in range(1, along)]
    peers += [before, after]
    barrier = pltpu.get_barrier_semaphore()
    for peer in peers:
        pl.semaphore_signal(barrier, inc=1, device_id=to(peer), device_id_type=MESH)

    loads = [
        (distances, dist_v), (w_rbf, rbf_v), (w_filter, filter_v),
        (features.at[:, 0:half], own.at[0, 0]), (features.at[:, half:width], own.at[0, 1]),
        (fractional, source_x.at[0]), (fractional, target_x.at[0]), (wave_index, wave_v),
        (neighbours, neigh_v), (edge_mask, mask_v), (w_mixing, mixing_v), (w_long, long_v),
        (w_short, short_v),
    ]
    loads = [pltpu.make_async_copy(x, y, in_sem.at[i]) for i, (x, y) in enumerate(loads)]
    for load in loads:
        load.start()

    def remote(source, target, send, recv, index):
        return pltpu.make_async_remote_copy(
            src_ref=source, dst_ref=target, send_sem=send, recv_sem=recv,
            device_id=to(index), device_id_type=MESH,
        )

    def send_states(layer):
        far = [
            remote(
                own.at[layer, 0], line_held.at[layer, k], line_send.at[layer, 0, k],
                line_recv.at[layer, 0, k], line(k),
            )
            for k in range(1, across)
        ] + [
            remote(
                own.at[layer, 1], plane_held.at[layer, k], plane_send.at[layer, 0, k],
                plane_recv.at[layer, 0, k], plane(k),
            )
            for k in range(1, along)
        ]
        near, cross = [], []
        for at, index in enumerate((after, before)):
            for part in range(2):
                copy = remote(
                    own.at[layer, part], beside.at[layer, at, part], near_send.at[layer, at, part],
                    near_recv.at[layer, at, part], index,
                )
                (cross if part else near).append(copy)
        for copy in far:
            copy.start()
        return near, cross, far

    first, last = b == 0, b == along - 1
    sends, takes = (last, first), (first, last)

    def start_near(near, cross):
        for at in range(2):
            near[at].start()
            pl.when(sends[at])(cross[at].start)

    def wait_near(near, cross):
        for at in range(2):
            near[at].wait_recv()
            pl.when(takes[at])(cross[at].wait_recv)

    def end_near(near, cross):
        for at in range(2):
            near[at].wait_send()
            pl.when(sends[at])(cross[at].wait_send)

    def transposed(x):
        return x.astype(jnp.float32).T.astype(jnp.bfloat16)

    center = 0.5 + 4.5 * lax.broadcasted_iota(jnp.int32, (count, rows), 0).astype(jnp.float32) / (
        count - 1
    )
    blocks = slots // GROUP

    def edge_weights(layer):
        rbf_t[layer] = transposed(rbf_v[layer].astype(jnp.float32) * 0.5)
        filter_t[layer] = transposed(filter_v[layer])

    def edge_filters(layer, begin, end):
        for first in range(begin * GROUP, end * GROUP, GROUP):
            parts = []
            for slot in range(first, first + GROUP):
                offset = dist_v[slot : slot + 1, :] - center
                parts.append(jnp.exp(-4.0 * offset * offset).astype(jnp.bfloat16))
            hidden_half = jnp.dot(
                rbf_t[layer], jnp.concatenate(parts, axis=1), preferred_element_type=jnp.float32
            )
            inner = (hidden_half + hidden_half * jnp.tanh(hidden_half)).astype(jnp.bfloat16)
            filters[layer, :, first * rows : (first + GROUP) * rows] = jnp.dot(
                filter_t[layer], inner, preferred_element_type=jnp.float32
            ).astype(jnp.bfloat16)

    place = lax.broadcasted_iota(jnp.int32, (3 * rows, rows), 0).astype(jnp.int16)

    def gather(layer, begin, end):
        total = message[...]
        for first in range(begin * GROUP, end * GROUP, GROUP):
            picks = []
            for slot in range(first, first + GROUP):
                hit = place == near16[slot : slot + 1, :]
                picks.append(jnp.where(hit, jnp.bfloat16(1), jnp.bfloat16(0)))
            gathered = jnp.dot(
                table[...], jnp.concatenate(picks, axis=1), preferred_element_type=jnp.float32
            )
            for at in range(GROUP):
                slot = first + at
                factor = filters[layer, :, slot * rows : (slot + 1) * rows].astype(jnp.float32)
                factor = factor * edge_v[slot : slot + 1, :]
                total = total + gathered[:, at * rows : (at + 1) * rows] * factor
        message[...] = total

    def send_partial(layer):
        copies = []

        def spread(block, held, parts, got, send, recv, target, order, blocks_out):
            product = jnp.dot(block, jnp.concatenate(held, axis=0), preferred_element_type=jnp.float32)
            for k in range(1, blocks_out):
                parts[layer, k] = product[k * rows : (k + 1) * rows, :].astype(jnp.bfloat16)
                copy = remote(
                    parts.at[layer, k], got.at[layer, k], send.at[layer, 1, k],
                    recv.at[layer, 1, k], target(k),
                )
                copy.start()
                copies.append(copy)
            own_field[order] = product[0:rows, :]

        spread(
            flipped[...],
            [own[layer, 1]] + [plane_held[layer, along - k] for k in range(1, along)],
            line_part, line_got, line_send, line_recv, lambda k: line(across - k), 1, across,
        )
        spread(
            matrix[...],
            [own[layer, 0]] + [line_held[layer, k] for k in range(1, across)],
            plane_part, plane_got, plane_send, plane_recv, plane, 0, along,
        )
        return copies

    def update(layer):
        short = jnp.dot(
            message[...].T.astype(jnp.bfloat16), short_v[layer], preferred_element_type=jnp.float32
        )
        left, right = own_field[0], own_field[1]
        for k in range(1, along):
            left = left + plane_got[layer, k].astype(jnp.float32)
        for k in range(1, across):
            right = right + line_got[layer, k].astype(jnp.float32)
        field = jnp.concatenate([left, right], axis=1).astype(jnp.bfloat16)
        step = short + jnp.dot(field, both[layer], preferred_element_type=jnp.float32)
        state = jnp.concatenate([own[layer, 0], own[layer, 1]], axis=1).astype(jnp.float32)
        return (state + step * jax.nn.sigmoid(step)).astype(jnp.bfloat16)

    def fill_table(layer):
        def put(at, part, ref):
            table[part * half : (part + 1) * half, at * rows : (at + 1) * rows] = transposed(ref[...])

        put(0, 0, beside.at[layer, 0, 0])
        put(1, 0, own.at[layer, 0])
        put(1, 1, own.at[layer, 1])
        put(2, 0, beside.at[layer, 1, 0])
        for at, slot in ((0, 1 % along), (1, along - 1)):
            pl.when(takes[at])(functools.partial(put, 2 * at, 1, beside.at[layer, at, 1]))
            pl.when(jnp.logical_not(takes[at]))(
                functools.partial(put, 2 * at, 1, plane_held.at[layer, slot])
            )

    done = [0] * (layers + 1)

    def fill(layer, end):
        if layer < layers and done[layer] < end:
            if done[layer] == 0:
                edge_weights(layer)
            edge_filters(layer, done[layer], end)
            done[layer] = end

    for load in loads[:3]:
        load.wait()
    fill(0, EARLY)
    for load in loads[3:7]:
        load.wait()
    pl.semaphore_wait(barrier, len(peers))
    placed_plane = [
        remote(target_x.at[0], target_x.at[k], place_send.at[1, k], place_recv.at[1, k], plane(k))
        for k in range(1, along)
    ]
    placed_line = [
        remote(source_x.at[0], source_x.at[k], place_send.at[0, k], place_recv.at[0, k], line(k))
        for k in range(1, across)
    ]
    for copy in placed_line + placed_plane:
        copy.start()
    near, cross, far = send_states(0)
    for load in loads[7:]:
        load.wait()
    weight = wave_weights(wave_v[...], scale)
    for m in range(-MOST, MOST + 1):
        weights[MOST + m] = jnp.broadcast_to(weight[:, 8 + m : 9 + m], (PAIRS, rows))
    for at, order in enumerate(pair_orders((PAIRS, rows))):
        orders[at] = order
    for row, (plain, weighted) in wave_rows(source_x[0], orders, weights):
        source_rows[row : row + plain.shape[0], 0:rows] = plain
        target_rows[row : row + plain.shape[0], 0:rows] = weighted
    fill(0, MIDDLE)
    start_near(near, cross)
    for layer in range(layers):
        both[layer] = jnp.dot(
            mixing_v[layer], long_v[layer], preferred_element_type=jnp.float32
        ).astype(jnp.bfloat16)
    near16[...] = neigh_v[...].astype(jnp.int16)
    envelope = 0.5 * (cos_sin(dist_v[...] * 0.1)[0] + 1.0)
    edge_v[...] = envelope * mask_v[...].astype(jnp.float32)
    fill(0, PRE)

    def lanes(k):
        if isinstance(k, int):
            return pl.ds(k * rows, rows)
        return pl.ds(pl.multiple_of(k * rows, rows), rows)

    def sources(k, carry):
        for row, (plain,) in wave_rows(source_x[k], orders, None):
            source_rows[row : row + plain.shape[0], lanes(k)] = plain
        return carry

    def targets(k, carry):
        for row, (_, weighted) in wave_rows(target_x[along - k], orders, weights):
            target_rows[row : row + weighted.shape[0], lanes(k)] = weighted
        return carry

    for copy in placed_plane:
        copy.wait_recv()
    lax.fori_loop(1, along, targets, 0)
    target_t[...] = target_rows[...].T
    for copy in placed_line:
        copy.wait_recv()
    middle = max(across // 2, 1)
    for first, last in ((0, middle), (middle, across)):
        for k in range(max(first, 1), last):
            sources(k, 0)
        product = jnp.dot(
            target_t[...], source_rows[:, first * rows : last * rows],
            preferred_element_type=jnp.float32,
        )
        matrix[:, first * rows : last * rows] = product.astype(jnp.bfloat16)
        flipped[first * rows : last * rows, :] = product.T.astype(jnp.bfloat16)

    sent = placed_line + placed_plane
    for layer in range(layers):
        message[...] = jnp.zeros_like(message)
        if layer > 0:
            fill(layer, min(done[layer] + LATER, blocks))
            start_near(near, cross)
            fill(layer, blocks)
        for copy in far:
            copy.wait_recv()
        copies = send_partial(layer)
        fill(layer, blocks)
        wait_near(near, cross)
        fill_table(layer)
        gather(layer, 0, blocks)
        fill(layer + 1, SECOND)
        for copy in copies:
            copy.wait_recv()
        sent += far + copies
        state = update(layer)
        end_near(near, cross)
        if layer + 1 < layers:
            own[layer + 1, 0] = state[:, 0:half]
            own[layer + 1, 1] = state[:, half:width]
            near, cross, far = send_states(layer + 1)
        else:
            out_ref[...] = state
    for copy in sent:
        copy.wait_send()


def per_device(
    features, fractional, distances, neighbours, edge_mask, wave_index,
    w_rbf, w_filter, w_mixing, w_short, w_long,
):
    bricks = lax.axis_size("atom")
    along = max(n for n in range(1, bricks + 1) if bricks % n == 0 and n * n <= bricks)
    across = bricks // along
    rows, width = features.shape
    slots = distances.shape[0]
    layers, count, hidden = w_rbf.shape
    scale = 4.0 / math.sqrt(wave_index.shape[1]) / math.sqrt(rows * bricks)
    waves = 2 * PAIRS * SIDE
    half, full = jnp.bfloat16, jnp.float32
    dma = pltpu.SemaphoreType.DMA
    V = pltpu.VMEM
    part = (rows, width // 2)
    scratch = [
        V(distances.shape, full), V(neighbours.shape, jnp.int32), V(edge_mask.shape, jnp.int32),
        V(wave_index.shape, jnp.int32), V(w_rbf.shape, half), V(w_filter.shape, half),
        V(w_mixing.shape, half), V(w_short.shape, half), V(w_long.shape, half),
        V((layers, hidden, count), half), V((layers, width, hidden), half),
        V((layers, width, width), half),
        V((2, PAIRS, rows), full), V((SIDE, PAIRS, rows), full), V((slots, rows), jnp.int16), V((slots, rows), full),
        V((across,) + fractional.shape, full), V((along,) + fractional.shape, full),
        V((waves, across * rows), half), V((waves, along * rows), half),
        V((along * rows, waves), half),
        V((along * rows, across * rows), half), V((across * rows, along * rows), half),
        V((layers, 2) + part, half), V((layers, 2, 2) + part, half),
        V((layers, across) + part, half), V((layers, along) + part, half),
        V((width, 3 * rows), half), V((layers, width, slots * rows), half),
        V((layers, along) + part, half), V((layers, across) + part, half),
        V((layers, along) + part, half), V((layers, across) + part, half),
        V((2,) + part, full), V((width, rows), full),
        dma((13,)), dma((layers, 2, 2)), dma((layers, 2, 2)),
        dma((layers, 2, across)), dma((layers, 2, across)),
        dma((layers, 2, along)), dma((layers, 2, along)),
        dma((2, max(across, along))), dma((2, max(across, along))),
    ]
    return pl.pallas_call(
        functools.partial(step_kernel, (across, along), scale),
        out_shape=pltpu.VMEM(features.shape, features.dtype),
        in_specs=[pl.BlockSpec(memory_space=pl.ANY)] * 11,
        out_specs=pl.BlockSpec(memory_space=pltpu.VMEM),
        scratch_shapes=scratch,
        compiler_params=pltpu.CompilerParams(
            collective_id=0, has_side_effects=True, vmem_limit_bytes=60 << 20
        ),
        name="step",
    )(
        features, fractional, distances, neighbours, edge_mask, wave_index,
        w_rbf, w_filter, w_mixing, w_short, w_long,
    )


def solution(mesh):
    split_rows = P(("rep", "atom"), None)
    split_columns = P(None, ("rep", "atom"))
    in_specs = (split_rows,) + (split_columns,) * 4 + (P(),) * 6
    return jax.shard_map(
        per_device, mesh=mesh, in_specs=in_specs, out_specs=split_rows, check_vma=False
    )
```

```python
import functools
import math

import jax
import jax.numpy as jnp
import numpy as np
from jax import lax
from jax.experimental import pallas as pl
from jax.experimental.pallas import tpu as pltpu
from jax.sharding import PartitionSpec as P

MOST = 6
PAIRS = 88
SIDE = 2 * MOST + 1
GROUP = 8
EARLY, MIDDLE, PRE, SECOND, LATER, TURN = 1, 3, 5, 0, 3, 3
MESH = pl.DeviceIdType.MESH


def fitted(function, terms):
    at = np.cos(np.pi * (np.arange(400) + 0.5) / 400) * 0.125 + 0.125
    values = function(np.sqrt(at))
    series = np.polynomial.chebyshev.Chebyshev.fit(at, values, terms - 1, domain=[0.0, 0.25])
    return [float(c) for c in series.convert(kind=np.polynomial.Polynomial).coef]


COS = fitted(lambda r: np.cos(2 * np.pi * r), 9)
SIN = fitted(lambda r: np.sin(2 * np.pi * r) / r, 8)


def horner(coefficients, x):
    total = jnp.full_like(x, coefficients[-1])
    for c in coefficients[-2::-1]:
        total = total * x + c
    return total


def cos_sin(turn):
    r = turn - jnp.floor(turn + 0.5)
    square = r * r
    return horner(COS, square), horner(SIN, square) * r


def pair_orders(shape):
    p = lax.broadcasted_iota(jnp.int32, shape, 0).astype(jnp.float32)
    row = jnp.floor((p - (MOST + 0.5)) * (1.0 / SIDE))
    m0 = row + 1.0
    m1 = jnp.where(m0 > 0.5, p - (MOST + 1) - row * SIDE - MOST, p)
    return m0, m1


def wave_weights(wave, scale):
    m0, m1, m2 = wave[0:1, :], wave[1:2, :], wave[2:3, :]
    flip = (m0 < 0) | ((m0 == 0) & (m1 < 0))
    m0, m1, m2 = (jnp.where(flip, -m, m) for m in (m0, m1, m2))
    pair = jnp.where(m0 == 0, m1, (MOST + 1) + (m0 - 1) * SIDE + m1 + MOST)
    many = wave.shape[1]
    one_pair = pair == lax.broadcasted_iota(jnp.int32, (PAIRS, many), 0)
    one_z = (m2 + 8) == lax.broadcasted_iota(jnp.int32, (16, many), 0)
    count = lax.dot_general(
        jnp.where(one_pair, 1.0, 0.0).astype(jnp.bfloat16),
        jnp.where(one_z, 1.0, 0.0).astype(jnp.bfloat16),
        (((1,), (1,)), ((), ())),
        preferred_element_type=jnp.float32,
    )
    n0, n1 = pair_orders((PAIRS, 16))
    n2 = lax.broadcasted_iota(jnp.int32, (PAIRS, 16), 1).astype(jnp.float32) - 8.0
    return count * scale / (1.0 + (n0 * n0 + n1 * n1 + n2 * n2) / 16.0)


def wave_rows(fraction, orders, weights):
    width = fraction.shape[1]
    cp, sp = cos_sin(orders[0] * fraction[0:1, :] + orders[1] * fraction[1:2, :])
    m2 = lax.broadcasted_iota(jnp.int32, (8, width), 0).astype(jnp.float32)
    cz, sz = cos_sin(m2 * fraction[2:3, :])
    for m in range(MOST + 1):
        if m == 0:
            signs, terms = (0, 0), (cp, sp)
        else:
            c, s = cz[m : m + 1, :], sz[m : m + 1, :]
            x, y, u, v = cp * c, sp * s, sp * c, cp * s
            signs, terms = (m, m, -m, -m), (x - y, u + v, x + y, u - v)
        row = 2 * PAIRS * max(2 * m - 1, 0)
        forms = [terms]
        if weights is not None:
            forms.append([weights[MOST + at] * term for at, term in zip(signs, terms)])
        yield row, [jnp.concatenate(form, axis=0).astype(jnp.bfloat16) for form in forms]


def step_kernel(
    grid, scale,
    features, fractional, distances, neighbours, edge_mask, wave_index,
    w_rbf, w_filter, w_mixing, w_short, w_long,
    out_ref,
    dist_v, neigh_v, mask_v, wave_v, rbf_v, filter_v, mixing_v, short_v, long_v,
    rbf_t, filter_t, both, orders, weights, near16, edge_v,
    source_x, target_x, source_rows, target_rows, target_t, matrix, flipped,
    own, beside, line_held, plane_held, table, filters,
    plane_part, line_part, plane_got, line_got, own_field, message,
    in_sem, near_send, near_recv, line_send, line_recv, plane_send, plane_recv,
    place_send, place_recv,
):
    across, along = grid
    bricks = across * along
    layers = w_rbf.shape[0]
    slots, rows = distances.shape
    count, hidden = w_rbf.shape[1:]
    width = w_filter.shape[2]
    half = width // 2
    me = lax.axis_index("atom")
    a, b = me // along, lax.rem(me, along)
    after = lax.rem(me + 1, bricks)
    before = lax.rem(me + bricks - 1, bricks)

    def line(k):
        return lax.rem(a + k, across) * along + b

    def plane(k):
        return a * along + lax.rem(b + k, along)

    def to(index):
        return {"atom": index}

    peers = [line(k) for k in range(1, across)] + [plane(k) for k in range(1, along)]
    peers += [before, after]
    barrier = pltpu.get_barrier_semaphore()
    for peer in peers:
        pl.semaphore_signal(barrier, inc=1, device_id=to(peer), device_id_type=MESH)

    loads = [
        (distances, dist_v), (w_rbf, rbf_v), (w_filter, filter_v),
        (features.at[:, 0:half], own.at[0, 0]), (features.at[:, half:width], own.at[0, 1]),
        (fractional, source_x.at[0]), (fractional, target_x.at[0]), (wave_index, wave_v),
        (neighbours, neigh_v), (edge_mask, mask_v), (w_mixing, mixing_v), (w_long, long_v),
        (w_short, short_v),
    ]
    loads = [pltpu.make_async_copy(x, y, in_sem.at[i]) for i, (x, y) in enumerate(loads)]
    for load in loads:
        load.start()

    def remote(source, target, send, recv, index):
        return pltpu.make_async_remote_copy(
            src_ref=source, dst_ref=target, send_sem=send, recv_sem=recv,
            device_id=to(index), device_id_type=MESH,
        )

    def send_states(layer):
        far = [
            remote(
                own.at[layer, 0], line_held.at[layer, k], line_send.at[layer, 0, k],
                line_recv.at[layer, 0, k], line(k),
            )
            for k in range(1, across)
        ] + [
            remote(
                own.at[layer, 1], plane_held.at[layer, k], plane_send.at[layer, 0, k],
                plane_recv.at[layer, 0, k], plane(k),
            )
            for k in range(1, along)
        ]
        near, cross = [], []
        for at, index in enumerate((after, before)):
            for part in range(2):
                copy = remote(
                    own.at[layer, part], beside.at[layer, at, part], near_send.at[layer, at, part],
                    near_recv.at[layer, at, part], index,
                )
                (cross if part else near).append(copy)
        for copy in far:
            copy.start()
        return near, cross, far

    first, last = b == 0, b == along - 1
    sends, takes = (last, first), (first, last)

    def start_near(near, cross):
        for at in range(2):
            near[at].start()
            pl.when(sends[at])(cross[at].start)

    def wait_near(near, cross):
        for at in range(2):
            near[at].wait_recv()
            pl.when(takes[at])(cross[at].wait_recv)

    def end_near(near, cross):
        for at in range(2):
            near[at].wait_send()
            pl.when(sends[at])(cross[at].wait_send)

    def transposed(x):
        return x.astype(jnp.float32).T.astype(jnp.bfloat16)

    center = 0.5 + 4.5 * lax.broadcasted_iota(jnp.int32, (count, rows), 0).astype(jnp.float32) / (
        count - 1
    )
    blocks = slots // GROUP

    def edge_weights(layer):
        rbf_t[layer] = transposed(rbf_v[layer].astype(jnp.float32) * 0.5)
        filter_t[layer] = transposed(filter_v[layer])

    def edge_filters(layer, begin, end):
        for first in range(begin * GROUP, end * GROUP, GROUP):
            parts = []
            for slot in range(first, first + GROUP):
                offset = dist_v[slot : slot + 1, :] - center
                parts.append(jnp.exp(-4.0 * offset * offset).astype(jnp.bfloat16))
            hidden_half = jnp.dot(
                rbf_t[layer], jnp.concatenate(parts, axis=1), preferred_element_type=jnp.float32
            )
            inner = (hidden_half + hidden_half * jnp.tanh(hidden_half)).astype(jnp.bfloat16)
            filters[layer, :, first * rows : (first + GROUP) * rows] = jnp.dot(
                filter_t[layer], inner, preferred_element_type=jnp.float32
            ).astype(jnp.bfloat16)

    place = lax.broadcasted_iota(jnp.int32, (3 * rows, rows), 0).astype(jnp.int16)

    def gather(layer, begin, end):
        total = message[...]
        for first in range(begin * GROUP, end * GROUP, GROUP):
            picks = []
            for slot in range(first, first + GROUP):
                hit = place == near16[slot : slot + 1, :]
                picks.append(jnp.where(hit, jnp.bfloat16(1), jnp.bfloat16(0)))
            gathered = jnp.dot(
                table[...], jnp.concatenate(picks, axis=1), preferred_element_type=jnp.float32
            )
            for at in range(GROUP):
                slot = first + at
                factor = filters[layer, :, slot * rows : (slot + 1) * rows].astype(jnp.float32)
                factor = factor * edge_v[slot : slot + 1, :]
                total = total + gathered[:, at * rows : (at + 1) * rows] * factor
        message[...] = total

    def send_partial(layer, far):
        copies = []
        far_line, far_plane = far[: across - 1], far[across - 1 :]

        def spread(block, held, parts, got, send, recv, target, order, blocks_out):
            product = jnp.dot(block, jnp.concatenate(held, axis=0), preferred_element_type=jnp.float32)
            for k in range(1, blocks_out):
                parts[layer, k] = product[k * rows : (k + 1) * rows, :].astype(jnp.bfloat16)
                copy = remote(
                    parts.at[layer, k], got.at[layer, k], send.at[layer, 1, k],
                    recv.at[layer, 1, k], target(k),
                )
                copy.start()
                copies.append(copy)
            own_field[order] = product[0:rows, :]

        for copy in far_plane:
            copy.wait_recv()
        spread(
            flipped[...],
            [own[layer, 1]] + [plane_held[layer, along - k] for k in range(1, along)],
            line_part, line_got, line_send, line_recv, lambda k: line(across - k), 1, across,
        )
        if layer > 0:
            fill(layer, blocks)
        for copy in far_line:
            copy.wait_recv()
        spread(
            matrix[...],
            [own[layer, 0]] + [line_held[layer, k] for k in range(1, across)],
            plane_part, plane_got, plane_send, plane_recv, plane, 0, along,
        )
        return copies

    def update(layer):
        short = jnp.dot(
            message[...].T.astype(jnp.bfloat16), short_v[layer], preferred_element_type=jnp.float32
        )
        left, right = own_field[0], own_field[1]
        for k in range(1, along):
            left = left + plane_got[layer, k].astype(jnp.float32)
        for k in range(1, across):
            right = right + line_got[layer, k].astype(jnp.float32)
        field = jnp.concatenate([left, right], axis=1).astype(jnp.bfloat16)
        step = short + jnp.dot(field, both[layer], preferred_element_type=jnp.float32)
        state = jnp.concatenate([own[layer, 0], own[layer, 1]], axis=1).astype(jnp.float32)
        return (state + step * jax.nn.sigmoid(step)).astype(jnp.bfloat16)

    def fill_table(layer):
        def put(at, part, ref):
            table[part * half : (part + 1) * half, at * rows : (at + 1) * rows] = transposed(ref[...])

        put(0, 0, beside.at[layer, 0, 0])
        put(1, 0, own.at[layer, 0])
        put(1, 1, own.at[layer, 1])
        put(2, 0, beside.at[layer, 1, 0])
        for at, slot in ((0, 1 % along), (1, along - 1)):
            pl.when(takes[at])(functools.partial(put, 2 * at, 1, beside.at[layer, at, 1]))
            pl.when(jnp.logical_not(takes[at]))(
                functools.partial(put, 2 * at, 1, plane_held.at[layer, slot])
            )

    done = [0] * (layers + 1)

    def fill(layer, end):
        if layer < layers and done[layer] < end:
            if done[layer] == 0:
                edge_weights(layer)
            edge_filters(layer, done[layer], end)
            done[layer] = end

    for load in loads[:3]:
        load.wait()
    fill(0, EARLY)
    for load in loads[3:7]:
        load.wait()
    pl.semaphore_wait(barrier, len(peers))
    placed_plane = [
        remote(target_x.at[0], target_x.at[k], place_send.at[1, k], place_recv.at[1, k], plane(k))
        for k in range(1, along)
    ]
    placed_line = [
        remote(source_x.at[0], source_x.at[k], place_send.at[0, k], place_recv.at[0, k], line(k))
        for k in range(1, across)
    ]
    for copy in placed_line + placed_plane:
        copy.start()
    near, cross, far = send_states(0)
    for load in loads[7:]:
        load.wait()
    weight = wave_weights(wave_v[...], scale)
    for m in range(-MOST, MOST + 1):
        weights[MOST + m] = jnp.broadcast_to(weight[:, 8 + m : 9 + m], (PAIRS, rows))
    for at, order in enumerate(pair_orders((PAIRS, rows))):
        orders[at] = order
    for row, (plain, weighted) in wave_rows(source_x[0], orders, weights):
        source_rows[row : row + plain.shape[0], 0:rows] = plain
        target_rows[row : row + plain.shape[0], 0:rows] = weighted
    fill(0, MIDDLE)
    start_near(near, cross)
    for layer in range(layers):
        both[layer] = jnp.dot(
            mixing_v[layer], long_v[layer], preferred_element_type=jnp.float32
        ).astype(jnp.bfloat16)
    near16[...] = neigh_v[...].astype(jnp.int16)
    envelope = 0.5 * (cos_sin(dist_v[...] * 0.1)[0] + 1.0)
    edge_v[...] = envelope * mask_v[...].astype(jnp.float32)
    fill(0, PRE)

    def lanes(k):
        if isinstance(k, int):
            return pl.ds(k * rows, rows)
        return pl.ds(pl.multiple_of(k * rows, rows), rows)

    def sources(k, carry):
        for row, (plain,) in wave_rows(source_x[k], orders, None):
            source_rows[row : row + plain.shape[0], lanes(k)] = plain
        return carry

    def targets(k, carry):
        for row, (_, weighted) in wave_rows(target_x[along - k], orders, weights):
            target_rows[row : row + weighted.shape[0], lanes(k)] = weighted
        return carry

    for copy in placed_plane:
        copy.wait_recv()
    lax.fori_loop(1, along, targets, 0)
    target_t[...] = target_rows[...].T
    for copy in placed_line:
        copy.wait_recv()
    middle = max(across // 2, 1)
    for first, last in ((0, middle), (middle, across)):
        for k in range(max(first, 1), last):
            sources(k, 0)
        product = jnp.dot(
            target_t[...], source_rows[:, first * rows : last * rows],
            preferred_element_type=jnp.float32,
        )
        matrix[:, first * rows : last * rows] = product.astype(jnp.bfloat16)
        flipped[first * rows : last * rows, :] = product.T.astype(jnp.bfloat16)

    sent = placed_line + placed_plane
    for layer in range(layers):
        message[...] = jnp.zeros_like(message)
        if layer > 0:
            fill(layer, min(done[layer] + LATER, blocks))
            start_near(near, cross)
            fill(layer, min(done[layer] + TURN, blocks))
        copies = send_partial(layer, far)
        fill(layer, blocks)
        wait_near(near, cross)
        fill_table(layer)
        gather(layer, 0, blocks)
        fill(layer + 1, SECOND)
        for copy in sent + far:
            copy.wait_send()
        end_near(near, cross)
        sent = copies
        for copy in copies:
            copy.wait_recv()
        state = update(layer)
        if layer + 1 < layers:
            own[layer + 1, 0] = state[:, 0:half]
            own[layer + 1, 1] = state[:, half:width]
            near, cross, far = send_states(layer + 1)
        else:
            out_ref[...] = state
    for copy in sent:
        copy.wait_send()


def per_device(
    features, fractional, distances, neighbours, edge_mask, wave_index,
    w_rbf, w_filter, w_mixing, w_short, w_long,
):
    bricks = lax.axis_size("atom")
    along = max(n for n in range(1, bricks + 1) if bricks % n == 0 and n * n <= bricks)
    across = bricks // along
    rows, width = features.shape
    slots = distances.shape[0]
    layers, count, hidden = w_rbf.shape
    scale = 4.0 / math.sqrt(wave_index.shape[1]) / math.sqrt(rows * bricks)
    waves = 2 * PAIRS * SIDE
    half, full = jnp.bfloat16, jnp.float32
    dma = pltpu.SemaphoreType.DMA
    V = pltpu.VMEM
    part = (rows, width // 2)
    scratch = [
        V(distances.shape, full), V(neighbours.shape, jnp.int32), V(edge_mask.shape, jnp.int32),
        V(wave_index.shape, jnp.int32), V(w_rbf.shape, half), V(w_filter.shape, half),
        V(w_mixing.shape, half), V(w_short.shape, half), V(w_long.shape, half),
        V((layers, hidden, count), half), V((layers, width, hidden), half),
        V((layers, width, width), half),
        V((2, PAIRS, rows), full), V((SIDE, PAIRS, rows), full), V((slots, rows), jnp.int16), V((slots, rows), full),
        V((across,) + fractional.shape, full), V((along,) + fractional.shape, full),
        V((waves, across * rows), half), V((waves, along * rows), half),
        V((along * rows, waves), half),
        V((along * rows, across * rows), half), V((across * rows, along * rows), half),
        V((layers, 2) + part, half), V((layers, 2, 2) + part, half),
        V((layers, across) + part, half), V((layers, along) + part, half),
        V((width, 3 * rows), half), V((layers, width, slots * rows), half),
        V((layers, along) + part, half), V((layers, across) + part, half),
        V((layers, along) + part, half), V((layers, across) + part, half),
        V((2,) + part, full), V((width, rows), full),
        dma((13,)), dma((layers, 2, 2)), dma((layers, 2, 2)),
        dma((layers, 2, across)), dma((layers, 2, across)),
        dma((layers, 2, along)), dma((layers, 2, along)),
        dma((2, max(across, along))), dma((2, max(across, along))),
    ]
    return pl.pallas_call(
        functools.partial(step_kernel, (across, along), scale),
        out_shape=pltpu.VMEM(features.shape, features.dtype),
        in_specs=[pl.BlockSpec(memory_space=pl.ANY)] * 11,
        out_specs=pl.BlockSpec(memory_space=pltpu.VMEM),
        scratch_shapes=scratch,
        compiler_params=pltpu.CompilerParams(
            collective_id=0, has_side_effects=True, vmem_limit_bytes=60 << 20
        ),
        name="step",
    )(
        features, fractional, distances, neighbours, edge_mask, wave_index,
        w_rbf, w_filter, w_mixing, w_short, w_long,
    )


def solution(mesh):
    split_rows = P(("rep", "atom"), None)
    split_columns = P(None, ("rep", "atom"))
    in_specs = (split_rows,) + (split_columns,) * 4 + (P(),) * 6
    return jax.shard_map(
        per_device, mesh=mesh, in_specs=in_specs, out_specs=split_rows, check_vma=False
    )
```

```python
import functools
import math

import jax
import jax.numpy as jnp
import numpy as np
from jax import lax
from jax.experimental import pallas as pl
from jax.experimental.pallas import tpu as pltpu
from jax.sharding import PartitionSpec as P

MOST = 6
PAIRS = 88
SIDE = 2 * MOST + 1
GROUP = 8
EARLY, MIDDLE, PRE, SECOND, LATER, TURN = 1, 3, 5, 0, 3, 3
MESH = pl.DeviceIdType.MESH


def fitted(function, terms):
    at = np.cos(np.pi * (np.arange(400) + 0.5) / 400) * 0.125 + 0.125
    values = function(np.sqrt(at))
    series = np.polynomial.chebyshev.Chebyshev.fit(at, values, terms - 1, domain=[0.0, 0.25])
    return [float(c) for c in series.convert(kind=np.polynomial.Polynomial).coef]


COS = fitted(lambda r: np.cos(2 * np.pi * r), 9)
SIN = fitted(lambda r: np.sin(2 * np.pi * r) / r, 8)


def horner(coefficients, x):
    total = jnp.full_like(x, coefficients[-1])
    for c in coefficients[-2::-1]:
        total = total * x + c
    return total


def cos_sin(turn):
    r = turn - jnp.floor(turn + 0.5)
    square = r * r
    return horner(COS, square), horner(SIN, square) * r


def pair_orders(shape):
    p = lax.broadcasted_iota(jnp.int32, shape, 0).astype(jnp.float32)
    row = jnp.floor((p - (MOST + 0.5)) * (1.0 / SIDE))
    m0 = row + 1.0
    m1 = jnp.where(m0 > 0.5, p - (MOST + 1) - row * SIDE - MOST, p)
    return m0, m1


def wave_weights(wave, scale):
    m0, m1, m2 = wave[0:1, :], wave[1:2, :], wave[2:3, :]
    flip = (m0 < 0) | ((m0 == 0) & (m1 < 0))
    m0, m1, m2 = (jnp.where(flip, -m, m) for m in (m0, m1, m2))
    pair = jnp.where(m0 == 0, m1, (MOST + 1) + (m0 - 1) * SIDE + m1 + MOST)
    many = wave.shape[1]
    one_pair = pair == lax.broadcasted_iota(jnp.int32, (PAIRS, many), 0)
    one_z = (m2 + 8) == lax.broadcasted_iota(jnp.int32, (16, many), 0)
    count = lax.dot_general(
        jnp.where(one_pair, 1.0, 0.0).astype(jnp.bfloat16),
        jnp.where(one_z, 1.0, 0.0).astype(jnp.bfloat16),
        (((1,), (1,)), ((), ())),
        preferred_element_type=jnp.float32,
    )
    n0, n1 = pair_orders((PAIRS, 16))
    n2 = lax.broadcasted_iota(jnp.int32, (PAIRS, 16), 1).astype(jnp.float32) - 8.0
    return count * scale / (1.0 + (n0 * n0 + n1 * n1 + n2 * n2) / 16.0)


def wave_rows(fraction, orders, weights):
    width = fraction.shape[1]
    cp, sp = cos_sin(orders[0] * fraction[0:1, :] + orders[1] * fraction[1:2, :])
    m2 = lax.broadcasted_iota(jnp.int32, (8, width), 0).astype(jnp.float32)
    cz, sz = cos_sin(m2 * fraction[2:3, :])
    for m in range(MOST + 1):
        if m == 0:
            signs, terms = (0, 0), (cp, sp)
        else:
            c, s = cz[m : m + 1, :], sz[m : m + 1, :]
            x, y, u, v = cp * c, sp * s, sp * c, cp * s
            signs, terms = (m, m, -m, -m), (x - y, u + v, x + y, u - v)
        row = 2 * PAIRS * max(2 * m - 1, 0)
        forms = [terms]
        if weights is not None:
            forms.append([weights[MOST + at] * term for at, term in zip(signs, terms)])
        yield row, [jnp.concatenate(form, axis=0).astype(jnp.bfloat16) for form in forms]


def step_kernel(
    grid, scale,
    features, fractional, distances, neighbours, edge_mask, wave_index,
    w_rbf, w_filter, w_mixing, w_short, w_long,
    out_ref,
    dist_v, neigh_v, mask_v, wave_v, rbf_v, filter_v, mixing_v, short_v, long_v,
    rbf_t, filter_t, both, orders, weights, near16, edge_v,
    source_x, target_x, source_rows, target_rows, target_t, matrix, flipped,
    own, beside, line_held, plane_held, table, filters,
    plane_part, line_part, plane_got, line_got, own_field, message,
    in_sem, near_send, near_recv, line_send, line_recv, plane_send, plane_recv,
    place_send, place_recv,
):
    across, along = grid
    bricks = across * along
    layers = w_rbf.shape[0]
    slots, rows = distances.shape
    count, hidden = w_rbf.shape[1:]
    width = w_filter.shape[2]
    half = width // 2
    me = lax.axis_index("atom")
    a, b = me // along, lax.rem(me, along)
    after = lax.rem(me + 1, bricks)
    before = lax.rem(me + bricks - 1, bricks)

    def line(k):
        return lax.rem(a + k, across) * along + b

    def plane(k):
        return a * along + lax.rem(b + k, along)

    def to(index):
        return {"atom": index}

    peers = [line(k) for k in range(1, across)] + [plane(k) for k in range(1, along)]
    peers += [before, after]
    barrier = pltpu.get_barrier_semaphore()
    for peer in peers:
        pl.semaphore_signal(barrier, inc=1, device_id=to(peer), device_id_type=MESH)

    loads = [
        (distances, dist_v), (w_rbf, rbf_v), (w_filter, filter_v),
        (features.at[:, 0:half], own.at[0, 0]), (features.at[:, half:width], own.at[0, 1]),
        (fractional, source_x.at[0]), (fractional, target_x.at[0]), (wave_index, wave_v),
        (neighbours, neigh_v), (edge_mask, mask_v), (w_mixing, mixing_v), (w_long, long_v),
        (w_short, short_v),
    ]
    loads = [pltpu.make_async_copy(x, y, in_sem.at[i]) for i, (x, y) in enumerate(loads)]
    for load in loads:
        load.start()

    def remote(source, target, send, recv, index):
        return pltpu.make_async_remote_copy(
            src_ref=source, dst_ref=target, send_sem=send, recv_sem=recv,
            device_id=to(index), device_id_type=MESH,
        )

    def send_states(layer):
        far = [
            remote(
                own.at[layer, 0], line_held.at[layer, k], line_send.at[layer, 0, k],
                line_recv.at[layer, 0, k], line(k),
            )
            for k in range(1, across)
        ] + [
            remote(
                own.at[layer, 1], plane_held.at[layer, k], plane_send.at[layer, 0, k],
                plane_recv.at[layer, 0, k], plane(k),
            )
            for k in range(1, along)
        ]
        near, cross = [], []
        for at, index in enumerate((after, before)):
            for part in range(2):
                copy = remote(
                    own.at[layer, part], beside.at[layer, at, part], near_send.at[layer, at, part],
                    near_recv.at[layer, at, part], index,
                )
                (cross if part else near).append(copy)
        for copy in far[across - 1 :] + far[: across - 1]:
            copy.start()
        return near, cross, far

    first, last = b == 0, b == along - 1
    sends, takes = (last, first), (first, last)

    def start_near(near, cross):
        for at in range(2):
            near[at].start()
            pl.when(sends[at])(cross[at].start)

    def wait_near(near, cross):
        for at in range(2):
            near[at].wait_recv()
            pl.when(takes[at])(cross[at].wait_recv)

    def end_near(near, cross):
        for at in range(2):
            near[at].wait_send()
            pl.when(sends[at])(cross[at].wait_send)

    def transposed(x):
        return x.astype(jnp.float32).T.astype(jnp.bfloat16)

    center = 0.5 + 4.5 * lax.broadcasted_iota(jnp.int32, (count, rows), 0).astype(jnp.float32) / (
        count - 1
    )
    blocks = slots // GROUP

    def edge_weights(layer):
        rbf_t[layer] = transposed(rbf_v[layer].astype(jnp.float32) * 0.5)
        filter_t[layer] = transposed(filter_v[layer])

    def edge_filters(layer, begin, end):
        for first in range(begin * GROUP, end * GROUP, GROUP):
            parts = []
            for slot in range(first, first + GROUP):
                offset = dist_v[slot : slot + 1, :] - center
                parts.append(jnp.exp(-4.0 * offset * offset).astype(jnp.bfloat16))
            hidden_half = jnp.dot(
                rbf_t[layer], jnp.concatenate(parts, axis=1), preferred_element_type=jnp.float32
            )
            inner = (hidden_half + hidden_half * jnp.tanh(hidden_half)).astype(jnp.bfloat16)
            filters[layer, :, first * rows : (first + GROUP) * rows] = jnp.dot(
                filter_t[layer], inner, preferred_element_type=jnp.float32
            ).astype(jnp.bfloat16)

    place = lax.broadcasted_iota(jnp.int32, (3 * rows, rows), 0).astype(jnp.int16)

    def gather(layer, begin, end):
        total = message[...]
        for first in range(begin * GROUP, end * GROUP, GROUP):
            picks = []
            for slot in range(first, first + GROUP):
                hit = place == near16[slot : slot + 1, :]
                picks.append(jnp.where(hit, jnp.bfloat16(1), jnp.bfloat16(0)))
            gathered = jnp.dot(
                table[...], jnp.concatenate(picks, axis=1), preferred_element_type=jnp.float32
            )
            for at in range(GROUP):
                slot = first + at
                factor = filters[layer, :, slot * rows : (slot + 1) * rows].astype(jnp.float32)
                factor = factor * edge_v[slot : slot + 1, :]
                total = total + gathered[:, at * rows : (at + 1) * rows] * factor
        message[...] = total

    def send_partial(layer, far):
        copies = []
        far_line, far_plane = far[: across - 1], far[across - 1 :]

        def spread(block, held, parts, got, send, recv, target, order, blocks_out):
            product = jnp.dot(block, jnp.concatenate(held, axis=0), preferred_element_type=jnp.float32)
            for k in range(1, blocks_out):
                parts[layer, k] = product[k * rows : (k + 1) * rows, :].astype(jnp.bfloat16)
                copy = remote(
                    parts.at[layer, k], got.at[layer, k], send.at[layer, 1, k],
                    recv.at[layer, 1, k], target(k),
                )
                copy.start()
                copies.append(copy)
            own_field[order] = product[0:rows, :]

        for copy in far_plane:
            copy.wait_recv()
        spread(
            flipped[...],
            [own[layer, 1]] + [plane_held[layer, along - k] for k in range(1, along)],
            line_part, line_got, line_send, line_recv, lambda k: line(across - k), 1, across,
        )
        if layer > 0:
            fill(layer, blocks)
        for copy in far_line:
            copy.wait_recv()
        spread(
            matrix[...],
            [own[layer, 0]] + [line_held[layer, k] for k in range(1, across)],
            plane_part, plane_got, plane_send, plane_recv, plane, 0, along,
        )
        return copies

    def update(layer):
        short = jnp.dot(
            message[...].T.astype(jnp.bfloat16), short_v[layer], preferred_element_type=jnp.float32
        )
        left, right = own_field[0], own_field[1]
        for k in range(1, along):
            left = left + plane_got[layer, k].astype(jnp.float32)
        for k in range(1, across):
            right = right + line_got[layer, k].astype(jnp.float32)
        field = jnp.concatenate([left, right], axis=1).astype(jnp.bfloat16)
        step = short + jnp.dot(field, both[layer], preferred_element_type=jnp.float32)
        state = jnp.concatenate([own[layer, 0], own[layer, 1]], axis=1).astype(jnp.float32)
        return (state + step * jax.nn.sigmoid(step)).astype(jnp.bfloat16)

    def put(at, part, ref):
        table[part * half : (part + 1) * half, at * rows : (at + 1) * rows] = transposed(ref[...])

    def own_table(layer):
        put(1, 0, own.at[layer, 0])
        put(1, 1, own.at[layer, 1])

    def fill_table(layer):
        put(0, 0, beside.at[layer, 0, 0])
        put(2, 0, beside.at[layer, 1, 0])
        for at, slot in ((0, 1 % along), (1, along - 1)):
            pl.when(takes[at])(functools.partial(put, 2 * at, 1, beside.at[layer, at, 1]))
            pl.when(jnp.logical_not(takes[at]))(
                functools.partial(put, 2 * at, 1, plane_held.at[layer, slot])
            )

    done = [0] * (layers + 1)

    def fill(layer, end):
        if layer < layers and done[layer] < end:
            if done[layer] == 0:
                edge_weights(layer)
            edge_filters(layer, done[layer], end)
            done[layer] = end

    for load in loads[:3]:
        load.wait()
    fill(0, EARLY)
    for load in loads[3:7]:
        load.wait()
    pl.semaphore_wait(barrier, len(peers))
    placed_plane = [
        remote(target_x.at[0], target_x.at[k], place_send.at[1, k], place_recv.at[1, k], plane(k))
        for k in range(1, along)
    ]
    placed_line = [
        remote(source_x.at[0], source_x.at[k], place_send.at[0, k], place_recv.at[0, k], line(k))
        for k in range(1, across)
    ]
    for copy in placed_line + placed_plane:
        copy.start()
    near, cross, far = send_states(0)
    for load in loads[7:]:
        load.wait()
    weight = wave_weights(wave_v[...], scale)
    for m in range(-MOST, MOST + 1):
        weights[MOST + m] = jnp.broadcast_to(weight[:, 8 + m : 9 + m], (PAIRS, rows))
    for at, order in enumerate(pair_orders((PAIRS, rows))):
        orders[at] = order
    for row, (plain, weighted) in wave_rows(source_x[0], orders, weights):
        source_rows[row : row + plain.shape[0], 0:rows] = plain
        target_rows[row : row + plain.shape[0], 0:rows] = weighted
    fill(0, MIDDLE)
    start_near(near, cross)
    for layer in range(layers):
        both[layer] = jnp.dot(
            mixing_v[layer], long_v[layer], preferred_element_type=jnp.float32
        ).astype(jnp.bfloat16)
    near16[...] = neigh_v[...].astype(jnp.int16)
    envelope = 0.5 * (cos_sin(dist_v[...] * 0.1)[0] + 1.0)
    edge_v[...] = envelope * mask_v[...].astype(jnp.float32)
    fill(0, PRE)

    def lanes(k):
        if isinstance(k, int):
            return pl.ds(k * rows, rows)
        return pl.ds(pl.multiple_of(k * rows, rows), rows)

    def sources(k, carry):
        for row, (plain,) in wave_rows(source_x[k], orders, None):
            source_rows[row : row + plain.shape[0], lanes(k)] = plain
        return carry

    def targets(k, carry):
        for row, (_, weighted) in wave_rows(target_x[along - k], orders, weights):
            target_rows[row : row + weighted.shape[0], lanes(k)] = weighted
        return carry

    for copy in placed_plane:
        copy.wait_recv()
    lax.fori_loop(1, along, targets, 0)
    target_t[...] = target_rows[...].T
    for copy in placed_line:
        copy.wait_recv()
    middle = max(across // 2, 1)
    for first, last in ((0, middle), (middle, across)):
        for k in range(max(first, 1), last):
            sources(k, 0)
        product = jnp.dot(
            target_t[...], source_rows[:, first * rows : last * rows],
            preferred_element_type=jnp.float32,
        )
        matrix[:, first * rows : last * rows] = product.astype(jnp.bfloat16)
        flipped[first * rows : last * rows, :] = product.T.astype(jnp.bfloat16)

    sent = placed_line + placed_plane
    for layer in range(layers):
        message[...] = jnp.zeros_like(message)
        if layer > 0:
            fill(layer, min(done[layer] + LATER, blocks))
            start_near(near, cross)
            fill(layer, min(done[layer] + TURN, blocks))
        copies = send_partial(layer, far)
        fill(layer, blocks)
        own_table(layer)
        wait_near(near, cross)
        fill_table(layer)
        gather(layer, 0, blocks)
        fill(layer + 1, SECOND)
        for copy in sent + far:
            copy.wait_send()
        end_near(near, cross)
        sent = copies
        for copy in copies:
            copy.wait_recv()
        state = update(layer)
        if layer + 1 < layers:
            own[layer + 1, 0] = state[:, 0:half]
            own[layer + 1, 1] = state[:, half:width]
            near, cross, far = send_states(layer + 1)
        else:
            out_ref[...] = state
    for copy in sent:
        copy.wait_send()


def per_device(
    features, fractional, distances, neighbours, edge_mask, wave_index,
    w_rbf, w_filter, w_mixing, w_short, w_long,
):
    bricks = lax.axis_size("atom")
    along = max(n for n in range(1, bricks + 1) if bricks % n == 0 and n * n <= bricks)
    across = bricks // along
    rows, width = features.shape
    slots = distances.shape[0]
    layers, count, hidden = w_rbf.shape
    scale = 4.0 / math.sqrt(wave_index.shape[1]) / math.sqrt(rows * bricks)
    waves = 2 * PAIRS * SIDE
    half, full = jnp.bfloat16, jnp.float32
    dma = pltpu.SemaphoreType.DMA
    V = pltpu.VMEM
    part = (rows, width // 2)
    scratch = [
        V(distances.shape, full), V(neighbours.shape, jnp.int32), V(edge_mask.shape, jnp.int32),
        V(wave_index.shape, jnp.int32), V(w_rbf.shape, half), V(w_filter.shape, half),
        V(w_mixing.shape, half), V(w_short.shape, half), V(w_long.shape, half),
        V((layers, hidden, count), half), V((layers, width, hidden), half),
        V((layers, width, width), half),
        V((2, PAIRS, rows), full), V((SIDE, PAIRS, rows), full), V((slots, rows), jnp.int16), V((slots, rows), full),
        V((across,) + fractional.shape, full), V((along,) + fractional.shape, full),
        V((waves, across * rows), half), V((waves, along * rows), half),
        V((along * rows, waves), half),
        V((along * rows, across * rows), half), V((across * rows, along * rows), half),
        V((layers, 2) + part, half), V((layers, 2, 2) + part, half),
        V((layers, across) + part, half), V((layers, along) + part, half),
        V((width, 3 * rows), half), V((layers, width, slots * rows), half),
        V((layers, along) + part, half), V((layers, across) + part, half),
        V((layers, along) + part, half), V((layers, across) + part, half),
        V((2,) + part, full), V((width, rows), full),
        dma((13,)), dma((layers, 2, 2)), dma((layers, 2, 2)),
        dma((layers, 2, across)), dma((layers, 2, across)),
        dma((layers, 2, along)), dma((layers, 2, along)),
        dma((2, max(across, along))), dma((2, max(across, along))),
    ]
    return pl.pallas_call(
        functools.partial(step_kernel, (across, along), scale),
        out_shape=pltpu.VMEM(features.shape, features.dtype),
        in_specs=[pl.BlockSpec(memory_space=pl.ANY)] * 11,
        out_specs=pl.BlockSpec(memory_space=pltpu.VMEM),
        scratch_shapes=scratch,
        compiler_params=pltpu.CompilerParams(
            collective_id=0, has_side_effects=True, vmem_limit_bytes=60 << 20
        ),
        name="step",
    )(
        features, fractional, distances, neighbours, edge_mask, wave_index,
        w_rbf, w_filter, w_mixing, w_short, w_long,
    )


def solution(mesh):
    split_rows = P(("rep", "atom"), None)
    split_columns = P(None, ("rep", "atom"))
    in_specs = (split_rows,) + (split_columns,) * 4 + (P(),) * 6
    return jax.shard_map(
        per_device, mesh=mesh, in_specs=in_specs, out_specs=split_rows, check_vma=False
    )
```
